256 devices in a mesh: line: 128 (over y, x, z_hi, core), view: 2 (over z_lo).
Axes of the slice: x: 4, y: 4, z: 8 (z_hi: 4, z_lo: 2; z = z_hi * 2 + z_lo), core: 2. Of those that a mesh axis runs over, the one named last changes fastest.
Arguments:
- light_field: bfloat16 [128, 8, 8, 8192], P('line', None, 'view'), may hold values from -6 to 6
- query_weight: bfloat16 [2, 64, 128], replicated, may hold values from -0.75 to 0.75
- key_weight: bfloat16 [2, 64, 128], replicated, may hold values from -24 to 24
- value_weight: bfloat16 [2, 64, 128], replicated, may hold values from -0.75 to 0.75
- out_weight: bfloat16 [2, 128, 64], replicated, may hold values from -0.5 to 0.5
- conv_first: bfloat16 [3, 3, 64, 64], replicated, may hold values from -0.25 to 0.25
- conv_second: bfloat16 [3, 3, 64, 64], replicated, may hold values from -0.25 to 0.25
Outputs:
- result: bfloat16 [128, 8, 8, 8192], P('line', None, 'view')
The draws below stay inside these ranges and needn't reach their ends.
All inputs are finite; a program needn't handle non-finite values.
Results may differ from the reference program's by a relative error of at most 0.0069.
Values may be sent and summed in bfloat16 or wider, within the bound.
A program may use at most 64 MiB of HBM per device.

```python
import math
import jax
import jax.numpy as jnp
from jax import lax

UVIEWS = 8
VVIEWS = 8
CHANNELS = 64
ATTN_WIDTH = 128
COLS = 128
ROWS = 128


def paired_weights(key):
    folded = jax.random.fold_in(key, 11)
    first_key, second_key = jax.random.split(folded)
    deviation = CHANNELS ** (-0.5)
    query_part = jnp.clip(jax.random.normal(first_key, (2, CHANNELS, ATTN_WIDTH), jnp.float32) * deviation, -0.75, 0.75)
    fresh_noise = jnp.clip(jax.random.normal(second_key, (2, CHANNELS, ATTN_WIDTH), jnp.float32) * deviation, -0.75, 0.75)
    key_part = fresh_noise
    return (query_part, jnp.clip(key_part, -24.0, 24.0))


def draw_query_weight(key, part):
    return paired_weights(key)[0].astype(jnp.bfloat16)


def draw_key_weight(key, part):
    return paired_weights(key)[1].astype(jnp.bfloat16)


def shard_levels(key, shape, cuts, low, top_value):
    loudness = 1.0
    for axis_at, blocks in cuts:
        heights = jax.random.uniform(jax.random.fold_in(jax.random.fold_in(key, 6), axis_at), (blocks,), jnp.float32, low / len(cuts), top_value / len(cuts))
        loudness = loudness * jnp.repeat(jnp.exp(heights), shape[axis_at] // blocks).reshape((-1,) + (1,) * (len(shape) - 1 - axis_at))
    return loudness


def centred(key, extent, scale, bound, cuts=(), kind=jnp.bfloat16):
    values = scale * jax.random.normal(key, extent, jnp.float32)
    if cuts:
        values = values * shard_levels(key, extent, cuts, -0.22, 0.18)
    return jnp.clip(values, -bound, bound).astype(kind)


def setup_inputs(seed: int = 0) -> dict:
    splits = jax.random.split(jax.random.key(seed), 8)
    return {
        "light_field": centred(splits[0], (ROWS, UVIEWS, VVIEWS, COLS * CHANNELS), 1.0, 6.0, ((0, 128), (2, 2))),
        "query_weight": draw_query_weight(jax.random.fold_in(splits[7], 71), 0),
        "key_weight": draw_key_weight(jax.random.fold_in(splits[7], 71), 0),
        "value_weight": centred(splits[3], (2, CHANNELS, ATTN_WIDTH), CHANNELS ** -0.5, 0.75),
        "out_weight": centred(splits[4], (2, ATTN_WIDTH, CHANNELS), ATTN_WIDTH ** -0.5, 0.5),
        "conv_first": centred(splits[5], (3, 3, CHANNELS, CHANNELS), (9 * CHANNELS) ** -0.5, 0.25),
        "conv_second": centred(splits[6], (3, 3, CHANNELS, CHANNELS), (9 * CHANNELS) ** -0.5, 0.25),
    }


def layer_norm(tokens):
    values = tokens.astype(jnp.float32)
    centre = values - lax.optimization_barrier(jnp.mean(values, axis=-1, keepdims=True))
    spread = lax.optimization_barrier(jnp.mean(centre * centre, axis=-1, keepdims=True))
    return (centre * lax.rsqrt(spread + 1e-05)).astype(jnp.bfloat16)

def project(inputs, matrix):
    return jnp.dot(inputs, matrix, preferred_element_type=jnp.float32).astype(jnp.bfloat16)

def lines_attend(tokens, query_matrix, key_matrix, value_matrix, out_matrix):
    normed = layer_norm(tokens)
    queries = project(normed, query_matrix)
    keys = project(normed, key_matrix)
    values = project(normed, value_matrix)
    scaling = 1.0 / math.sqrt(queries.shape[-1])

    def per_line(operands):
        query_rows, key_rows, value_rows = operands
        scores = jnp.einsum('qa,ka->qk', query_rows.astype(jnp.float32), key_rows.astype(jnp.float32)) * scaling
        exponent = jnp.exp(scores - lax.optimization_barrier(jnp.max(scores, axis=-1, keepdims=True)))
        weights = (exponent / lax.optimization_barrier(jnp.sum(exponent, axis=-1, keepdims=True))).astype(jnp.bfloat16)
        return jnp.dot(weights, value_rows, preferred_element_type=jnp.float32).astype(jnp.bfloat16)
    mixed = lax.map(per_line, (queries, keys, values))
    summed = tokens.astype(jnp.float32) + jnp.dot(mixed, out_matrix, preferred_element_type=jnp.float32)
    return summed.astype(jnp.bfloat16)

def correlate(images, kernel):
    return lax.conv_general_dilated(images.astype(jnp.float32), kernel.astype(jnp.float32), (1, 1), 'SAME', dimension_numbers=('NHWC', 'HWIO', 'NHWC'), precision=lax.Precision.HIGHEST)

def leaky_relu(values):
    return jnp.where(values >= 0, values, 0.1 * values)

def reference(light_field, query_weight, key_weight, value_weight, out_weight, conv_first, conv_second):
    ray_grid = light_field.reshape(ROWS, UVIEWS, VVIEWS, COLS, CHANNELS)
    horizontal = ray_grid.transpose(0, 2, 1, 3, 4).reshape(ROWS * VVIEWS, UVIEWS * COLS, CHANNELS)
    after_rows = lines_attend(horizontal, query_weight[0], key_weight[0], value_weight[0], out_weight[0])
    after_rows = after_rows.reshape(ROWS, VVIEWS, UVIEWS, COLS, CHANNELS)
    vertical = after_rows.transpose(2, 3, 1, 0, 4).reshape(UVIEWS * COLS, VVIEWS * ROWS, CHANNELS)
    second = lines_attend(vertical, query_weight[1], key_weight[1], value_weight[1], out_weight[1])
    second = second.reshape(UVIEWS, COLS, VVIEWS, ROWS, CHANNELS)
    images = second.transpose(0, 2, 3, 1, 4).reshape(UVIEWS * VVIEWS, ROWS, COLS, CHANNELS)
    hidden = leaky_relu(correlate(images, conv_first)).astype(jnp.bfloat16)
    summed = (images.astype(jnp.float32) + correlate(hidden, conv_second)).astype(jnp.bfloat16)
    summed = summed.reshape(UVIEWS, VVIEWS, ROWS, COLS, CHANNELS).transpose(2, 0, 1, 3, 4)
    return summed.reshape(ROWS, UVIEWS, VVIEWS, COLS * CHANNELS)
```

```python
import functools
import math

import jax
import jax.numpy as jnp
from jax import lax
from jax.experimental import pallas as pl
from jax.experimental.pallas import tpu as pltpu
from jax.sharding import PartitionSpec as P

F32 = jnp.float32
BF16 = jnp.bfloat16
MESH = pl.DeviceIdType.MESH

XY = 16
ZC = 16
VL = 4
CH = 64
WIDTH = 128
SCALE2 = math.log2(math.e) / math.sqrt(WIDTH)
GROUP = 32
TOK = 1024


def fold(n, body):
    def step(i, carry):
        body(i)
        return carry

    lax.fori_loop(0, n, step, 0)


def normalise(x, avg):
    mean = jnp.dot(x, avg[0:WIDTH, :], preferred_element_type=F32)
    centre = x.astype(F32) - mean
    square = centre * centre
    high = square.astype(BF16)
    low = (square - high.astype(F32)).astype(BF16)
    spread = jnp.dot(
        jnp.concatenate([high, low], axis=1), avg[...], preferred_element_type=F32
    )
    return (centre * lax.rsqrt(spread + 1e-05)).astype(BF16)


def attend_block(line, at, q_s, k_s, va_s, m_s):
    scores = lax.dot_general(
        q_s[line, at, :], k_s[line], (((1,), (1,)), ((), ())), preferred_element_type=F32
    )
    top = jnp.max(scores, axis=1, keepdims=True)
    e = jnp.exp2((scores - top) * SCALE2).astype(BF16)
    o = jnp.dot(e, va_s[line], preferred_element_type=F32)
    m_s[line, at, :] = (o[:, :WIDTH] / o[:, WIDTH:]).astype(BF16)


def kernel(
    x_ref, wq_ref, wk_ref, wv_ref, wo_ref, c1_ref, c2_ref, out_ref,
    w_qkv, w_out, w_c1, w_c2, avg, perm, perm_in, perm_out,
    q_s, k_s, va_s, m_s,
    y_send, a_recv, b_send, r_recv,
    tok, pad, hid,
    b2_send, a2_recv, y2_send, f_recv,
    s_a, r_a, s_b, r_b, s_h, r_h, s_g, r_g, s_b2, r_b2, s_a2, r_a2,
):
    line = lax.axis_index("line")
    view = lax.axis_index("view")
    xy = line // 8
    zc = line % 8
    me = zc * 2 + view
    core = zc % 2
    z = (zc // 2) * 2 + view
    far_xy = (xy + 15 + 2 * core) % 16
    far = far_xy * 8 + zc + 1 - 2 * core
    near = line + 1 - 2 * core

    def z_peer(t):
        return (xy * 8 + t // 2, t % 2)

    def xy_peer(t):
        return (t * 8 + zc, view)

    barrier = pltpu.get_barrier_semaphore()

    def greet(d):
        pl.semaphore_signal(barrier, inc=1, device_id=z_peer((me + d + 1) % 16), device_id_type=MESH)
        pl.semaphore_signal(barrier, inc=1, device_id=xy_peer((xy + d + 1) % 16), device_id_type=MESH)

    fold(15, greet)
    pl.semaphore_signal(barrier, inc=1, device_id=(far, view), device_id_type=MESH)

    w_qkv[...] = jnp.zeros_like(w_qkv)
    w_out[...] = jnp.zeros_like(w_out)
    for i in range(2):
        for n, ref in enumerate((wq_ref, wk_ref, wv_ref)):
            for h in range(2):
                w_qkv[i, h * CH : (h + 1) * CH, (2 * n + h) * WIDTH : (2 * n + h + 1) * WIDTH] = ref[i]
        none = jnp.zeros((WIDTH, CH), BF16)
        w_out[i, 0:WIDTH, :] = jnp.concatenate([wo_ref[i], none], axis=1)
        w_out[i, WIDTH:, :] = jnp.concatenate([none, wo_ref[i]], axis=1)
    row = lax.broadcasted_iota(jnp.int32, (WIDTH, WIDTH), 0)
    col = lax.broadcasted_iota(jnp.int32, (WIDTH, WIDTH), 1)
    same = jnp.where((row < CH) == (col < CH), 1.0 / CH, 0.0).astype(BF16)
    avg[0:WIDTH, :] = same
    avg[WIDTH:, :] = same
    row = lax.broadcasted_iota(jnp.int32, (256, 256), 0)
    col = lax.broadcasted_iota(jnp.int32, (256, 256), 1)
    perm[...] = jnp.where(
        jnp.logical_and(row // 16 == col % 16, row % 16 == col // 16), 1.0, 0.0
    ).astype(BF16)
    for ref, a, b in ((perm_in, row, col), (perm_out, col, row)):
        here = jnp.logical_and(a // 32 == (b // 2) % 8, (a // 2) % 16 == b // 16)
        ref[...] = jnp.where(jnp.logical_and(here, a % 2 == b % 2), 1.0, 0.0).astype(BF16)
    for ln in range(4):
        va_s[ln, :, WIDTH:] = jnp.ones((TOK, WIDTH), BF16)

    def project_to(i, pair, where):
        normed = normalise(pair, avg)
        rows = pair.shape[0]
        qkv = jnp.dot(normed, w_qkv[i], preferred_element_type=F32).astype(BF16)
        for h, (ln, start) in enumerate(where):
            at = pl.ds(start, rows)
            q_s[ln, at, :] = qkv[:, h * WIDTH : (h + 1) * WIDTH]
            k_s[ln, at, :] = qkv[:, (2 + h) * WIDTH : (3 + h) * WIDTH]
            va_s[ln, at, 0:WIDTH] = qkv[:, (4 + h) * WIDTH : (5 + h) * WIDTH]

    def horizontal(v):
        for p in range(2):
            project_to(
                0, x_ref[v, :, p * WIDTH : (p + 1) * WIDTH],
                [(0, 2 * p * 256), (0, (2 * p + 1) * 256)],
            )
        for b in range(4):
            attend_block(0, slice(b * 256, (b + 1) * 256), q_s, k_s, va_s, m_s)
        for p in range(2):
            lanes = slice(p * WIDTH, (p + 1) * WIDTH)
            mixed = jnp.concatenate(
                [m_s[0, 2 * p * 256 : (2 * p + 1) * 256, :], m_s[0, (2 * p + 1) * 256 : (2 * p + 2) * 256, :]],
                axis=1,
            )
            added = jnp.dot(mixed, w_out[0], preferred_element_type=F32)
            y_send[v, :, lanes] = (x_ref[v, :, lanes].astype(F32) + added).astype(BF16)

    def send_z(src, dst, v, s_sem, r_sem):
        pltpu.make_async_copy(src.at[v, pl.ds(me * 16, 16), :], dst.at[v, me], r_sem.at[v]).start()

        def one(d):
            j = d // 2
            there = (z + 8 + (4 - (j + 1) // 2) * (2 * (j % 2) - 1)) % 8
            t = (there // 2) * 4 + ((core + d + 1) % 2) * 2 + there % 2
            pltpu.make_async_remote_copy(
                src_ref=src.at[v, pl.ds(t * 16, 16), :], dst_ref=dst.at[v, me],
                send_sem=s_sem.at[v], recv_sem=r_sem.at[v],
                device_id=z_peer(t), device_id_type=MESH,
            ).start()

        fold(15, one)

    def send_xy(src, dst, v, s_sem, r_sem):
        pltpu.make_async_copy(src.at[v, pl.ds(xy * 16, 16), :], dst.at[v, xy], r_sem.at[v]).start()

        def one(d):
            t = (xy + d + 1) % 16
            pltpu.make_async_remote_copy(
                src_ref=src.at[v, pl.ds(t * 16, 16), :], dst_ref=dst.at[v, xy],
                send_sem=s_sem.at[v], recv_sem=r_sem.at[v],
                device_id=xy_peer(t), device_id_type=MESH,
            ).start()

        fold(15, one)

    def wait_all(ref, v, sem):
        pltpu.make_async_copy(ref.at[v], ref.at[v], sem.at[v]).wait()

    def wait_sent(ref, v, sem):
        part = ref.at[v, pl.ds(0, 15)]
        pltpu.make_async_copy(part, part, sem.at[v]).wait()

    def reorder(src, dst, v):
        rows = jnp.concatenate([src[v, s] for s in range(16)], axis=0)
        dst[v] = jnp.dot(perm[...], rows, preferred_element_type=F32).astype(BF16)

    def forward(v):
        wait_all(a_recv, v, r_a)
        reorder(a_recv, b_send, v)
        send_xy(b_send, r_recv, v, s_b, r_b)

    horizontal(0)
    pl.semaphore_wait(barrier, 31)
    send_z(y_send, a_recv, 0, s_a, r_a)

    horizontal(1)
    send_z(y_send, a_recv, 1, s_a, r_a)

    def rows_step(i):
        horizontal(i + 2)
        send_z(y_send, a_recv, i + 2, s_a, r_a)
        forward(i)

    fold(VL - 2, rows_step)

    w_c1[...] = jnp.zeros_like(w_c1)
    w_c2[...] = jnp.zeros_like(w_c2)
    none = jnp.zeros((CH, CH), BF16)
    for ref, dst, outs, shift in ((c1_ref, w_c1, 4, 0), (c2_ref, w_c2, 2, 1)):
        for dy in range(3):
            for d in (-1, 0, 1):
                if d == -1:
                    rows = [[none, none], [ref[dy, 0], none]]
                elif d == 0:
                    rows = [[ref[dy, 1], ref[dy, 0]], [ref[dy, 2], ref[dy, 1]]]
                else:
                    rows = [[none, ref[dy, 2]], [none, none]]
                tile = jnp.concatenate([jnp.concatenate(r, axis=1) for r in rows], axis=0)
                for po in range(outs):
                    pi = po + shift + d
                    if 0 <= pi < 4:
                        dst[
                            dy * 512 + pi * WIDTH : dy * 512 + (pi + 1) * WIDTH,
                            po * WIDTH : (po + 1) * WIDTH,
                        ] = tile

    def columns(v):
        wait_all(r_recv, v, r_b)
        rows = jnp.concatenate([r_recv[v, s] for s in range(16)], axis=0)
        tok[v] = jnp.dot(perm_in[...], rows, preferred_element_type=F32).astype(BF16)
        at = pl.multiple_of(v * 256, 256)
        for p in range(2):
            project_to(
                1, tok[v, :, p * WIDTH : (p + 1) * WIDTH], [(2 * p, at), (2 * p + 1, at)]
            )

    forward(2)
    fold(2, columns)
    forward(3)
    fold(2, lambda i: columns(i + 2))

    def attend_pair(p, v):
        at = pl.ds(pl.multiple_of(v * 256, 256), 256)
        for h in range(2):
            attend_block(2 * p + h, at, q_s, k_s, va_s, m_s)

    inner = slice(GROUP, GROUP + 256)

    def join(v):
        at = pl.ds(pl.multiple_of(v * 256, 256), 256)
        for p in range(2):
            mixed = jnp.concatenate([m_s[2 * p, at, :], m_s[2 * p + 1, at, :]], axis=1)
            added = jnp.dot(mixed, w_out[1], preferred_element_type=F32)
            x = tok[v, :, p * WIDTH : (p + 1) * WIDTH].astype(F32)
            pad[v, p + 1, inner, :] = (x + added).astype(BF16)

    left = jnp.where(core == 0, far, near)
    right = jnp.where(core == 0, near, far)

    def halos(v):
        return (
            pltpu.make_async_remote_copy(
                src_ref=pad.at[v, 1, inner, :], dst_ref=pad.at[v, 3, inner, :],
                send_sem=s_h.at[v], recv_sem=r_h.at[v],
                device_id=(left, view), device_id_type=MESH,
            ),
            pltpu.make_async_remote_copy(
                src_ref=pad.at[v, 2, inner, :], dst_ref=pad.at[v, 0, inner, :],
                send_sem=s_g.at[v], recv_sem=r_g.at[v],
                device_id=(right, view), device_id_type=MESH,
            ),
        )

    block = xy * 2 + core
    has_left = jnp.where(block == 0, 0.0, 1.0).astype(F32)
    has_right = jnp.where(block == 31, 0.0, 1.0).astype(F32)
    place = lax.broadcasted_iota(jnp.int32, (GROUP, WIDTH), 0)

    def rims(ref):
        for p in range(4):
            last = pltpu.roll(ref[p, 8 * GROUP : 9 * GROUP, :].astype(F32), 2, 0)
            ref[p, 0:GROUP, :] = jnp.where(place < 2, 0.0, last).astype(BF16)
            head = pltpu.roll(ref[p, GROUP : 2 * GROUP, :].astype(F32), GROUP - 2, 0)
            ref[p, 9 * GROUP :, :] = jnp.where(place >= GROUP - 2, 0.0, head).astype(BF16)

    def taps(ref):
        return jnp.concatenate(
            [ref[p, dy * GROUP : dy * GROUP + 256, :] for dy in range(3) for p in range(4)], axis=1
        )

    def convolve(v):
        for copy in halos(v):
            copy.wait()
        here = pad.at[v]
        here[0, inner, :] = (here[0, inner, :].astype(F32) * has_left).astype(BF16)
        here[3, inner, :] = (here[3, inner, :].astype(F32) * has_right).astype(BF16)
        rims(here)
        got = jnp.dot(taps(here), w_c1[...], preferred_element_type=F32)
        got = jnp.where(got >= 0, got, 0.1 * got)
        hid[0, inner, :] = (got[:, 0:WIDTH] * has_left).astype(BF16)
        hid[1, inner, :] = got[:, WIDTH : 2 * WIDTH].astype(BF16)
        hid[2, inner, :] = got[:, 2 * WIDTH : 3 * WIDTH].astype(BF16)
        hid[3, inner, :] = (got[:, 3 * WIDTH :] * has_right).astype(BF16)
        rims(hid)
        got = jnp.dot(taps(hid), w_c2[...], preferred_element_type=F32)
        second = jnp.concatenate([here[1, inner, :], here[2, inner, :]], axis=1)
        result = (second.astype(F32) + got).astype(BF16)
        b2_send[v] = jnp.dot(perm_out[...], result, preferred_element_type=F32).astype(BF16)
        send_xy(b2_send, a2_recv, v, s_b2, r_b2)

    def back(v):
        wait_all(a2_recv, v, r_b2)
        reorder(a2_recv, y2_send, v)
        send_z(y2_send, f_recv, v, s_a2, r_a2)

    def start_halos(v):
        attend_pair(1, v)
        join(v)
        for copy in halos(v):
            copy.start()

    attend_pair(0, 0)
    start_halos(0)
    attend_pair(0, 1)
    convolve(0)

    def columns_step(i):
        start_halos(i + 1)
        attend_pair(0, i + 2)
        convolve(i + 1)
        back(i)

    fold(2, columns_step)
    start_halos(3)
    convolve(3)
    back(2)
    back(3)

    def arrive(v):
        wait_all(f_recv, v, r_a2)
        out_ref[v] = f_recv[v]

    fold(VL, arrive)

    def drain(v):
        wait_sent(a_recv, v, s_a)
        wait_sent(r_recv, v, s_b)
        wait_sent(a2_recv, v, s_b2)
        wait_sent(f_recv, v, s_a2)

    fold(VL, drain)


def local(light_field, query_weight, key_weight, value_weight, out_weight, conv_first, conv_second):
    x = light_field.reshape(4, 2, VL, XY, 2, 256).transpose(2, 0, 4, 1, 3, 5)
    x = x.reshape(VL, 256, 256)
    vmem = pl.BlockSpec(memory_space=pltpu.VMEM)
    grid4 = pltpu.VMEM((VL, 16, 16, 256), BF16)
    flat4 = pltpu.VMEM((VL, 256, 256), BF16)
    sem = pltpu.SemaphoreType.DMA((VL,))
    got = pl.pallas_call(
        kernel,
        out_shape=jax.ShapeDtypeStruct((VL, 16, 16, 256), BF16),
        in_specs=[vmem] * 7,
        out_specs=vmem,
        scratch_shapes=[
            pltpu.VMEM((2, WIDTH, 6 * WIDTH), BF16),
            pltpu.VMEM((2, 2 * WIDTH, WIDTH), BF16),
            pltpu.VMEM((1536, 512), BF16),
            pltpu.VMEM((1536, 256), BF16),
            pltpu.VMEM((2 * WIDTH, WIDTH), BF16),
            pltpu.VMEM((256, 256), BF16),
            pltpu.VMEM((256, 256), BF16),
            pltpu.VMEM((256, 256), BF16),
            pltpu.VMEM((4, TOK, WIDTH), BF16),
            pltpu.VMEM((4, TOK, WIDTH), BF16),
            pltpu.VMEM((4, TOK, 2 * WIDTH), BF16),
            pltpu.VMEM((4, TOK, WIDTH), BF16),
            flat4, grid4, flat4, grid4,
            flat4,
            pltpu.VMEM((VL, 4, 10 * GROUP, WIDTH), BF16),
            pltpu.VMEM((4, 10 * GROUP, WIDTH), BF16),
            flat4, grid4, flat4, grid4,
            sem, sem, sem, sem, sem, sem, sem, sem, sem, sem, sem, sem,
        ],
        compiler_params=pltpu.CompilerParams(
            collective_id=0, has_side_effects=True, vmem_limit_bytes=48 << 20
        ),
    )(x, query_weight, key_weight, value_weight, out_weight, conv_first, conv_second)
    got = got.reshape(VL, 4, 2, 2, XY, 256).transpose(1, 3, 0, 4, 2, 5)
    return got.reshape(1, 8, VL, 8192)


def solution(mesh):
    placed = (P("line", None, "view", None), P(), P(), P(), P(), P(), P())
    return jax.shard_map(
        local, mesh=mesh, in_specs=placed, out_specs=P("line", None, "view", None), check_vma=False
    )
```

```python
import functools
import math

import jax
import jax.numpy as jnp
from jax import lax
from jax.experimental import pallas as pl
from jax.experimental.pallas import tpu as pltpu
from jax.sharding import PartitionSpec as P

F32 = jnp.float32
BF16 = jnp.bfloat16
MESH = pl.DeviceIdType.MESH

XY = 16
ZC = 16
VL = 4
CH = 64
WIDTH = 128
SCALE2 = math.log2(math.e) / math.sqrt(WIDTH)
GROUP = 32
TOK = 1024


def snake(t):
    y = t // 4
    x = t % 4
    return 4 * y + x + (y % 2) * (3 - 2 * x)


def fold(n, body):
    def step(i, carry):
        body(i)
        return carry

    lax.fori_loop(0, n, step, 0)


def normalise(x, avg):
    mean = jnp.dot(x, avg[0:WIDTH, :], preferred_element_type=F32)
    centre = x.astype(F32) - mean
    square = centre * centre
    high = square.astype(BF16)
    low = (square - high.astype(F32)).astype(BF16)
    spread = jnp.dot(
        jnp.concatenate([high, low], axis=1), avg[...], preferred_element_type=F32
    )
    return (centre * lax.rsqrt(spread + 1e-05)).astype(BF16)


def attend_block(line, at, q_s, k_s, va_s, m_s):
    scores = lax.dot_general(
        q_s[line, at, :], k_s[line], (((1,), (1,)), ((), ())), preferred_element_type=F32
    )
    top = jnp.max(scores, axis=1, keepdims=True)
    e = jnp.exp2((scores - top) * SCALE2).astype(BF16)
    o = jnp.dot(e, va_s[line], preferred_element_type=F32)
    m_s[line, at, :] = (o[:, :WIDTH] / o[:, WIDTH:]).astype(BF16)


def kernel(
    x_hbm, wq_hbm, wk_hbm, wv_hbm, wo_hbm, c1_hbm, c2_hbm, out_ref,
    x_in, wq_ref, wk_ref, wv_ref, wo_ref, c1_ref, c2_ref, x_rows,
    w_qkv, w_out, w_c1, w_c2, avg, perm, perm_in, perm_out, perm_end,
    q_s, k_s, va_s, m_s,
    y_send, a_recv, b_send, r_recv,
    tok, pad, hid,
    b2_send, a2_recv, y2_send, f_recv,
    l_sem, s_a, r_a, s_b, r_b, s_h, r_h, s_g, r_g, s_b2, r_b2, s_a2, r_a2,
):
    line = lax.axis_index("line")
    view = lax.axis_index("view")
    xy = line // 8
    zc = line % 8
    me = zc * 2 + view
    core = zc % 2
    z = (zc // 2) * 2 + view
    place_xy = snake(xy)
    far_xy = snake((place_xy + 15 + 2 * core) % 16)
    far = far_xy * 8 + zc + 1 - 2 * core
    near = line + 1 - 2 * core

    def z_peer(t):
        return (xy * 8 + t // 2, t % 2)

    def xy_peer(t):
        return (t * 8 + zc, view)

    barrier = pltpu.get_barrier_semaphore()

    def greet(d):
        pl.semaphore_signal(barrier, inc=1, device_id=z_peer((me + d + 1) % 16), device_id_type=MESH)
        pl.semaphore_signal(barrier, inc=1, device_id=xy_peer((xy + d + 1) % 16), device_id_type=MESH)

    fold(15, greet)
    pl.semaphore_signal(barrier, inc=1, device_id=(far, view), device_id_type=MESH)

    loads = [
        pltpu.make_async_copy(src, dst, l_sem.at[i])
        for i, (src, dst) in enumerate(
            (
                (x_hbm, x_in), (wq_hbm, wq_ref), (wk_hbm, wk_ref), (wv_hbm, wv_ref),
                (wo_hbm, wo_ref), (c1_hbm, c1_ref), (c2_hbm, c2_ref),
            )
        )
    ]
    for load in loads:
        load.start()
    for load in loads:
        load.wait()

    w_qkv[...] = jnp.zeros_like(w_qkv)
    w_out[...] = jnp.zeros_like(w_out)
    for i in range(2):
        for n, ref in enumerate((wq_ref, wk_ref, wv_ref)):
            for h in range(2):
                w_qkv[i, h * CH : (h + 1) * CH, (2 * n + h) * WIDTH : (2 * n + h + 1) * WIDTH] = ref[i]
        w_out[i, 0:CH, 0:WIDTH] = wo_ref[i]
        w_out[i, CH:, WIDTH:] = wo_ref[i]
    row = lax.broadcasted_iota(jnp.int32, (WIDTH, WIDTH), 0)
    col = lax.broadcasted_iota(jnp.int32, (WIDTH, WIDTH), 1)
    same = jnp.where((row < CH) == (col < CH), 1.0 / CH, 0.0).astype(BF16)
    avg[0:WIDTH, :] = same
    avg[WIDTH:, :] = same
    row = lax.broadcasted_iota(jnp.int32, (256, 256), 0)
    col = lax.broadcasted_iota(jnp.int32, (256, 256), 1)
    perm[...] = jnp.where(
        jnp.logical_and(row // 16 == col % 16, row % 16 == col // 16), 1.0, 0.0
    ).astype(BF16)
    for ref, a, b in ((perm_in, row, col), (perm_out, col, row)):
        for odd in range(2):
            if odd:
                here = jnp.logical_and(a // 32 == b // 32, (a // 2) % 16 == b % 16)
                here = jnp.logical_and(here, a % 2 == (b // 16) % 2)
            else:
                here = jnp.logical_and(a // 32 == (b // 2) % 8, (a // 2) % 16 == b // 16)
                here = jnp.logical_and(here, a % 2 == b % 2)
            ref[odd] = jnp.where(here, 1.0, 0.0).astype(BF16)
    chip = snake(row % 16)
    for odd in range(2):
        if odd:
            here = jnp.logical_and(col % 16 == chip, col // 16 == row // 16)
        else:
            here = jnp.logical_and(col // 16 == chip, col % 16 == row // 16)
        perm_end[odd] = jnp.where(here, 1.0, 0.0).astype(BF16)
    for ln in range(4):
        va_s[ln, :, WIDTH:] = jnp.ones((TOK, WIDTH), BF16)

    w_c1[...] = jnp.zeros_like(w_c1)
    w_c2[...] = jnp.zeros_like(w_c2)
    none = jnp.zeros((CH, CH), BF16)
    for ref, dst, outs, shift in ((c1_ref, w_c1, 4, 0), (c2_ref, w_c2, 2, 1)):
        for dy in range(3):
            for d in (-1, 0, 1):
                if d == -1:
                    rows = [[none, none], [ref[dy, 0], none]]
                elif d == 0:
                    rows = [[ref[dy, 1], ref[dy, 0]], [ref[dy, 2], ref[dy, 1]]]
                else:
                    rows = [[none, ref[dy, 2]], [none, none]]
                tile = jnp.concatenate([jnp.concatenate(r, axis=1) for r in rows], axis=0)
                for po in range(outs):
                    pi = po + shift + d
                    if 0 <= pi < 4:
                        dst[
                            dy * 512 + pi * WIDTH : dy * 512 + (pi + 1) * WIDTH,
                            po * WIDTH : (po + 1) * WIDTH,
                        ] = tile

    def bring(t):
        for d in range(16):
            start = pl.multiple_of(snake(t) * 512 + (d // 2) % 2 * 256, 256)
            rays = x_in[(d // 4) * 2 + d % 2, :, pl.ds(start, 256)].astype(F32)
            for p in range(2):
                x_rows[p, pl.ds(d * 16 + t, VL, stride=256), :] = rays[:, p * WIDTH : (p + 1) * WIDTH]

    fold(16, bring)

    def project_to(i, pair, where):
        normed = normalise(pair, avg)
        rows = pair.shape[0]
        qkv = jnp.dot(normed, w_qkv[i], preferred_element_type=F32).astype(BF16)
        for h, (ln, start) in enumerate(where):
            at = pl.ds(start, rows)
            q_s[ln, at, :] = qkv[:, h * WIDTH : (h + 1) * WIDTH]
            k_s[ln, at, :] = qkv[:, (2 + h) * WIDTH : (3 + h) * WIDTH]
            va_s[ln, at, 0:WIDTH] = qkv[:, (4 + h) * WIDTH : (5 + h) * WIDTH]

    def out_project(i, mixed):
        return lax.dot_general(
            mixed, w_out[i], (((1,), (1,)), ((), ())), preferred_element_type=F32
        )

    def horizontal(v):
        at = pl.ds(pl.multiple_of(v * 256, 256), 256)
        for p in range(2):
            project_to(
                0, x_rows[p, at, :].astype(BF16), [(0, 2 * p * 256), (0, (2 * p + 1) * 256)]
            )
        for b in range(4):
            attend_block(0, slice(b * 256, (b + 1) * 256), q_s, k_s, va_s, m_s)
        for p in range(2):
            mixed = jnp.concatenate(
                [m_s[0, 2 * p * 256 : (2 * p + 1) * 256, :], m_s[0, (2 * p + 1) * 256 : (2 * p + 2) * 256, :]],
                axis=1,
            )
            added = out_project(0, mixed)
            y_send[v, :, p * WIDTH : (p + 1) * WIDTH] = (x_rows[p, at, :] + added).astype(BF16)

        @pl.when(v % 2 == 1)
        def _():
            y_send[v] = jnp.dot(perm[...], y_send[v], preferred_element_type=F32).astype(BF16)

    def send_z(src, dst, v, s_sem, r_sem):
        pltpu.make_async_copy(src.at[v, pl.ds(me * 16, 16), :], dst.at[v, me], r_sem.at[v]).start()

        def one(d):
            j = d // 2
            there = (z + 8 + (4 - (j + 1) // 2) * (2 * (j % 2) - 1)) % 8
            t = (there // 2) * 4 + ((core + d + 1) % 2) * 2 + there % 2
            pltpu.make_async_remote_copy(
                src_ref=src.at[v, pl.ds(t * 16, 16), :], dst_ref=dst.at[v, me],
                send_sem=s_sem.at[v], recv_sem=r_sem.at[v],
                device_id=z_peer(t), device_id_type=MESH,
            ).start()

        fold(15, one)

    def send_xy(src, dst, v, s_sem, r_sem):
        pltpu.make_async_copy(src.at[v, pl.ds(xy * 16, 16), :], dst.at[v, xy], r_sem.at[v]).start()

        def one(d):
            t = (xy + d + 1) % 16
            pltpu.make_async_remote_copy(
                src_ref=src.at[v, pl.ds(t * 16, 16), :], dst_ref=dst.at[v, xy],
                send_sem=s_sem.at[v], recv_sem=r_sem.at[v],
                device_id=xy_peer(t), device_id_type=MESH,
            ).start()

        fold(15, one)

    def wait_all(ref, v, sem):
        pltpu.make_async_copy(ref.at[v], ref.at[v], sem.at[v]).wait()

    def wait_sent(ref, v, sem):
        part = ref.at[v, pl.ds(0, 15)]
        pltpu.make_async_copy(part, part, sem.at[v]).wait()

    def reorder(src, dst, v):
        rows = jnp.concatenate([src[v, s] for s in range(16)], axis=0)
        dst[v] = jnp.dot(perm[...], rows, preferred_element_type=F32).astype(BF16)

    def first_stage(along_z, src, dst, v, s_sem, r_sem):
        @pl.when(along_z)
        def _():
            send_z(src, dst, v, s_sem, r_sem)

        @pl.when(jnp.logical_not(along_z))
        def _():
            send_xy(src, dst, v, s_sem, r_sem)

    def start(v):
        first_stage(v % 2 == 0, y_send, a_recv, v, s_a, r_a)

    def forward(v):
        wait_all(a_recv, v, r_a)
        reorder(a_recv, b_send, v)
        first_stage(v % 2 == 1, b_send, r_recv, v, s_b, r_b)

    def rows_step(v):
        horizontal(v)

        @pl.when(v == 1)
        def _():
            pl.semaphore_wait(barrier, 31)
            start(0)

        @pl.when(v > 0)
        def _():
            start(v)

    fold(VL, rows_step)
    fold(VL, lambda i: forward(i + 1 - 2 * (i % 2)))

    def columns(v):
        wait_all(r_recv, v, r_b)
        rows = jnp.concatenate([r_recv[v, s] for s in range(16)], axis=0)
        tok[v] = jnp.dot(perm_in[v % 2], rows, preferred_element_type=F32).astype(BF16)
        at = pl.multiple_of(v * 256, 256)
        for p in range(2):
            project_to(
                1, tok[v, :, p * WIDTH : (p + 1) * WIDTH], [(2 * p, at), (2 * p + 1, at)]
            )

    fold(VL, columns)

    inner = slice(GROUP, GROUP + 256)

    def attend(v):
        at = pl.ds(pl.multiple_of(v * 256, 256), 256)
        for ln in range(4):
            attend_block(ln, at, q_s, k_s, va_s, m_s)
        for p in range(2):
            mixed = jnp.concatenate([m_s[2 * p, at, :], m_s[2 * p + 1, at, :]], axis=1)
            added = out_project(1, mixed)
            x = tok[v, :, p * WIDTH : (p + 1) * WIDTH].astype(F32)
            pad[v, p + 1, inner, :] = (x + added).astype(BF16)
        for copy in halos(v):
            copy.start()

    left = jnp.where(core == 0, far, near)
    right = jnp.where(core == 0, near, far)

    def halos(v):
        return (
            pltpu.make_async_remote_copy(
                src_ref=pad.at[v, 1, inner, :], dst_ref=pad.at[v, 3, inner, :],
                send_sem=s_h.at[v], recv_sem=r_h.at[v],
                device_id=(left, view), device_id_type=MESH,
            ),
            pltpu.make_async_remote_copy(
                src_ref=pad.at[v, 2, inner, :], dst_ref=pad.at[v, 0, inner, :],
                send_sem=s_g.at[v], recv_sem=r_g.at[v],
                device_id=(right, view), device_id_type=MESH,
            ),
        )

    block = place_xy * 2 + core
    has_left = jnp.where(block == 0, 0.0, 1.0).astype(F32)
    has_right = jnp.where(block == 31, 0.0, 1.0).astype(F32)
    place = lax.broadcasted_iota(jnp.int32, (GROUP, WIDTH), 0)

    def rims(ref):
        for p in range(4):
            last = pltpu.roll(ref[p, 8 * GROUP : 9 * GROUP, :].astype(F32), 2, 0)
            ref[p, 0:GROUP, :] = jnp.where(place < 2, 0.0, last).astype(BF16)
            head = pltpu.roll(ref[p, GROUP : 2 * GROUP, :].astype(F32), GROUP - 2, 0)
            ref[p, 9 * GROUP :, :] = jnp.where(place >= GROUP - 2, 0.0, head).astype(BF16)

    def taps(ref):
        return jnp.concatenate(
            [ref[p, dy * GROUP : dy * GROUP + 256, :] for dy in range(3) for p in range(4)], axis=1
        )

    def convolve(v):
        for copy in halos(v):
            copy.wait()
        here = pad.at[v]
        here[0, inner, :] = (here[0, inner, :].astype(F32) * has_left).astype(BF16)
        here[3, inner, :] = (here[3, inner, :].astype(F32) * has_right).astype(BF16)
        rims(here)
        got = jnp.dot(taps(here), w_c1[...], preferred_element_type=F32)
        got = jnp.where(got >= 0, got, 0.1 * got)
        hid[0, inner, :] = (got[:, 0:WIDTH] * has_left).astype(BF16)
        hid[1, inner, :] = got[:, WIDTH : 2 * WIDTH].astype(BF16)
        hid[2, inner, :] = got[:, 2 * WIDTH : 3 * WIDTH].astype(BF16)
        hid[3, inner, :] = (got[:, 3 * WIDTH :] * has_right).astype(BF16)
        rims(hid)
        got = jnp.dot(taps(hid), w_c2[...], preferred_element_type=F32)
        second = jnp.concatenate([here[1, inner, :], here[2, inner, :]], axis=1)
        result = (second.astype(F32) + got).astype(BF16)
        late = v // 3
        b2_send[v] = jnp.dot(perm_out[1 - late], result, preferred_element_type=F32).astype(BF16)
        first_stage(v < 3, b2_send, a2_recv, v, s_b2, r_b2)

    def back(v):
        wait_all(a2_recv, v, r_b2)
        reorder(a2_recv, y2_send, v)
        first_stage(v == 3, y2_send, f_recv, v, s_a2, r_a2)

    def columns_step(i):
        @pl.when(i < VL)
        def _():
            attend(i)

        @pl.when(i > 0)
        def _():
            convolve(i - 1)

    fold(VL + 1, columns_step)
    fold(VL, lambda i: back(i + i // 2 - 3 * (i // 3) + i // 3))

    def arrive(v):
        wait_all(f_recv, v, r_a2)
        rows = jnp.concatenate([f_recv[v, s] for s in range(16)], axis=0)
        got = jnp.dot(perm_end[v // 3], rows, preferred_element_type=F32).astype(BF16)
        for s in range(16):
            out_ref[v, s] = got[s * 16 : (s + 1) * 16, :]

    fold(VL, arrive)

    def drain(v):
        wait_sent(a_recv, v, s_a)
        wait_sent(r_recv, v, s_b)
        wait_sent(a2_recv, v, s_b2)
        wait_sent(f_recv, v, s_a2)

    fold(VL, drain)


def local(light_field, query_weight, key_weight, value_weight, out_weight, conv_first, conv_second):
    x = light_field.reshape(8, VL, 8192)
    vmem = pl.BlockSpec(memory_space=pltpu.VMEM)
    grid4 = pltpu.VMEM((VL, 16, 16, 256), BF16)
    flat4 = pltpu.VMEM((VL, 256, 256), BF16)
    sem = pltpu.SemaphoreType.DMA((VL,))
    weight = pltpu.VMEM((2, CH, WIDTH), BF16)
    taps = pltpu.VMEM((3, 3, CH, CH), BF16)
    got = pl.pallas_call(
        kernel,
        out_shape=jax.ShapeDtypeStruct((VL, 16, 16, 256), BF16),
        in_specs=[pl.BlockSpec(memory_space=pltpu.MemorySpace.HBM)] * 7,
        out_specs=vmem,
        scratch_shapes=[
            pltpu.VMEM((8, VL, 8192), BF16),
            weight, weight, weight, weight, taps, taps,
            pltpu.VMEM((2, TOK, WIDTH), F32),
            pltpu.VMEM((2, WIDTH, 6 * WIDTH), BF16),
            pltpu.VMEM((2, WIDTH, 2 * WIDTH), BF16),
            pltpu.VMEM((1536, 512), BF16),
            pltpu.VMEM((1536, 256), BF16),
            pltpu.VMEM((2 * WIDTH, WIDTH), BF16),
            pltpu.VMEM((256, 256), BF16),
            pltpu.VMEM((2, 256, 256), BF16),
            pltpu.VMEM((2, 256, 256), BF16),
            pltpu.VMEM((2, 256, 256), BF16),
            pltpu.VMEM((4, TOK, WIDTH), BF16),
            pltpu.VMEM((4, TOK, WIDTH), BF16),
            pltpu.VMEM((4, TOK, 2 * WIDTH), BF16),
            pltpu.VMEM((4, TOK, WIDTH), BF16),
            flat4, grid4, flat4, grid4,
            flat4,
            pltpu.VMEM((VL, 4, 10 * GROUP, WIDTH), BF16),
            pltpu.VMEM((4, 10 * GROUP, WIDTH), BF16),
            flat4, grid4, flat4, grid4,
            pltpu.SemaphoreType.DMA((7,)),
            sem, sem, sem, sem, sem, sem, sem, sem, sem, sem, sem, sem,
        ],
        compiler_params=pltpu.CompilerParams(
            collective_id=0, has_side_effects=True, vmem_limit_bytes=48 << 20
        ),
    )(x, query_weight, key_weight, value_weight, out_weight.transpose(0, 2, 1), conv_first, conv_second)
    got = got.reshape(VL, 4, 2, 2, XY, 256).transpose(1, 3, 0, 4, 2, 5)
    return got.reshape(1, 8, VL, 8192)


def solution(mesh):
    placed = (P("line", None, "view", None), P(), P(), P(), P(), P(), P())
    return jax.shard_map(
        local, mesh=mesh, in_specs=placed, out_specs=P("line", None, "view", None), check_vma=False
    )
```

```python
import functools
import math

import jax
import jax.numpy as jnp
from jax import lax
from jax.experimental import pallas as pl
from jax.experimental.pallas import tpu as pltpu
from jax.sharding import PartitionSpec as P

F32 = jnp.float32
BF16 = jnp.bfloat16
MESH = pl.DeviceIdType.MESH

XY = 16
ZC = 16
VL = 4
CH = 64
WIDTH = 128
SCALE2 = math.log2(math.e) / math.sqrt(WIDTH)
GROUP = 32
TOK = 1024


def snake(t):
    y = t // 4
    x = t % 4
    return 4 * y + x + (y % 2) * (3 - 2 * x)


def fold(n, body):
    def step(i, carry):
        body(i)
        return carry

    lax.fori_loop(0, n, step, 0)


def normalise(x, avg):
    mean = jnp.dot(x, avg[0:WIDTH, :], preferred_element_type=F32)
    centre = x.astype(F32) - mean
    square = centre * centre
    high = square.astype(BF16)
    low = (square - high.astype(F32)).astype(BF16)
    spread = jnp.dot(
        jnp.concatenate([high, low], axis=1), avg[...], preferred_element_type=F32
    )
    return (centre * lax.rsqrt(spread + 1e-05)).astype(BF16)


def attend_block(line, at, q_s, k_s, va_s, m_s):
    scores = lax.dot_general(
        q_s[line, at, :], k_s[line], (((1,), (1,)), ((), ())), preferred_element_type=F32
    )
    top = jnp.max(scores, axis=1, keepdims=True)
    e = jnp.exp2((scores - top) * SCALE2).astype(BF16)
    o = jnp.dot(e, va_s[line], preferred_element_type=F32)
    m_s[line, at, :] = (o[:, :WIDTH] / o[:, WIDTH:]).astype(BF16)


def kernel(
    x_hbm, wq_hbm, wk_hbm, wv_hbm, wo_hbm, c1_hbm, c2_hbm, out_ref,
    x_in, wq_ref, wk_ref, wv_ref, wo_ref, c1_ref, c2_ref, x_rows,
    w_qkv, w_out, w_c1, w_c1b, w_c2, avg, perm, perm_in, perm_out, perm_end,
    q_s, k_s, va_s, m_s,
    y_send, a_recv, b_send, r_recv,
    tok, pad, hid,
    b2_send, a2_recv, y2_send, f_recv,
    l_sem, s_a, r_a, s_b, r_b, s_h, r_h, s_g, r_g, s_b2, r_b2, s_a2, r_a2,
):
    line = lax.axis_index("line")
    view = lax.axis_index("view")
    xy = line // 8
    zc = line % 8
    me = zc * 2 + view
    core = zc % 2
    z = (zc // 2) * 2 + view
    place_xy = snake(xy)
    far_xy = snake((place_xy + 15 + 2 * core) % 16)
    far = far_xy * 8 + zc + 1 - 2 * core
    near = line + 1 - 2 * core

    def z_peer(t):
        return (xy * 8 + t // 2, t % 2)

    def xy_peer(t):
        return (t * 8 + zc, view)

    def z_order(d):
        j = d // 2
        there = (z + 8 + (4 - (j + 1) // 2) * (2 * (j % 2) - 1)) % 8
        return (there // 2) * 4 + ((core + d + 1) % 2) * 2 + there % 2

    def hop(j):
        return (2 - j + (j // 2) * (2 * j - 1)) % 4

    def xy_order(d):
        return ((xy // 4 + hop(d // 4)) % 4) * 4 + (xy % 4 + hop(d % 4)) % 4

    barrier = pltpu.get_barrier_semaphore()

    def greet(d):
        pl.semaphore_signal(barrier, inc=1, device_id=z_peer(z_order(d)), device_id_type=MESH)
        pl.semaphore_signal(barrier, inc=1, device_id=xy_peer(xy_order(d)), device_id_type=MESH)

    fold(15, greet)
    pl.semaphore_signal(barrier, inc=1, device_id=(far, view), device_id_type=MESH)

    loads = [
        pltpu.make_async_copy(src, dst, l_sem.at[i])
        for i, (src, dst) in enumerate(
            (
                (x_hbm, x_in), (wq_hbm, wq_ref), (wk_hbm, wk_ref), (wv_hbm, wv_ref),
                (wo_hbm, wo_ref), (c1_hbm, c1_ref), (c2_hbm, c2_ref),
            )
        )
    ]
    for load in loads:
        load.start()
    for load in loads:
        load.wait()

    w_qkv[...] = jnp.zeros_like(w_qkv)
    w_out[...] = jnp.zeros_like(w_out)
    for i in range(2):
        for n, ref in enumerate((wq_ref, wk_ref, wv_ref)):
            for h in range(2):
                w_qkv[i, h * CH : (h + 1) * CH, (2 * n + h) * WIDTH : (2 * n + h + 1) * WIDTH] = ref[i]
        w_out[i, 0:CH, 0:WIDTH] = wo_ref[i]
        w_out[i, CH:, WIDTH:] = wo_ref[i]
    row = lax.broadcasted_iota(jnp.int32, (WIDTH, WIDTH), 0)
    col = lax.broadcasted_iota(jnp.int32, (WIDTH, WIDTH), 1)
    same = jnp.where((row < CH) == (col < CH), 1.0 / CH, 0.0).astype(BF16)
    avg[0:WIDTH, :] = same
    avg[WIDTH:, :] = same
    row = lax.broadcasted_iota(jnp.int32, (256, 256), 0)
    col = lax.broadcasted_iota(jnp.int32, (256, 256), 1)
    perm[...] = jnp.where(
        jnp.logical_and(row // 16 == col % 16, row % 16 == col // 16), 1.0, 0.0
    ).astype(BF16)
    for ref, a, b in ((perm_in, row, col), (perm_out, col, row)):
        for odd in range(2):
            if odd:
                here = jnp.logical_and(a // 32 == b // 32, (a // 2) % 16 == b % 16)
                here = jnp.logical_and(here, a % 2 == (b // 16) % 2)
            else:
                here = jnp.logical_and(a // 32 == (b // 2) % 8, (a // 2) % 16 == b // 16)
                here = jnp.logical_and(here, a % 2 == b % 2)
            ref[odd] = jnp.where(here, 1.0, 0.0).astype(BF16)
    chip = snake(row % 16)
    for odd in range(2):
        if odd:
            here = jnp.logical_and(col % 16 == chip, col // 16 == row // 16)
        else:
            here = jnp.logical_and(col // 16 == chip, col % 16 == row // 16)
        perm_end[odd] = jnp.where(here, 1.0, 0.0).astype(BF16)
    for ln in range(4):
        va_s[ln, :, WIDTH:] = jnp.ones((TOK, WIDTH), BF16)

    none = jnp.zeros((CH, CH), BF16)
    for ref, dst, ins, outs in (
        (c1_ref, w_c1, range(-2, 4), range(-1, 3)),
        (c1_ref, w_c1b, range(2, 6), range(3, 5)),
        (c2_ref, w_c2, range(-1, 5), range(0, 4)),
    ):
        for dy in range(3):
            for i, c in enumerate(ins):
                row0 = (dy * len(ins) + i) * CH
                dst[row0 : row0 + CH, :] = jnp.concatenate(
                    [ref[dy, c - o + 1] if 0 <= c - o + 1 <= 2 else none for o in outs], axis=1
                )

    def bring(t):
        for d in range(16):
            start = pl.multiple_of(snake(t) * 512 + (d // 2) % 2 * 256, 256)
            rays = x_in[(d // 4) * 2 + d % 2, :, pl.ds(start, 256)].astype(F32)
            for p in range(2):
                x_rows[p, pl.ds(d * 16 + t, VL, stride=256), :] = rays[:, p * WIDTH : (p + 1) * WIDTH]

    fold(16, bring)

    def project_to(i, pair, where):
        normed = normalise(pair, avg)
        rows = pair.shape[0]
        qkv = jnp.dot(normed, w_qkv[i], preferred_element_type=F32).astype(BF16)
        for h, (ln, start) in enumerate(where):
            at = pl.ds(start, rows)
            q_s[ln, at, :] = qkv[:, h * WIDTH : (h + 1) * WIDTH]
            k_s[ln, at, :] = qkv[:, (2 + h) * WIDTH : (3 + h) * WIDTH]
            va_s[ln, at, 0:WIDTH] = qkv[:, (4 + h) * WIDTH : (5 + h) * WIDTH]

    def out_project(i, mixed):
        return lax.dot_general(
            mixed, w_out[i], (((1,), (1,)), ((), ())), preferred_element_type=F32
        )

    def horizontal(v):
        at = pl.ds(pl.multiple_of(v * 256, 256), 256)
        for p in range(2):
            project_to(
                0, x_rows[p, at, :].astype(BF16), [(0, 2 * p * 256), (0, (2 * p + 1) * 256)]
            )
        for b in range(4):
            attend_block(0, slice(b * 256, (b + 1) * 256), q_s, k_s, va_s, m_s)
        for p in range(2):
            mixed = jnp.concatenate(
                [m_s[0, 2 * p * 256 : (2 * p + 1) * 256, :], m_s[0, (2 * p + 1) * 256 : (2 * p + 2) * 256, :]],
                axis=1,
            )
            added = out_project(0, mixed)
            y_send[v, :, p * WIDTH : (p + 1) * WIDTH] = (x_rows[p, at, :] + added).astype(BF16)

        @pl.when(v % 2 == 1)
        def _():
            y_send[v] = jnp.dot(perm[...], y_send[v], preferred_element_type=F32).astype(BF16)

    def send_z(src, dst, v, s_sem, r_sem):
        pltpu.make_async_copy(src.at[v, pl.ds(me * 16, 16), :], dst.at[v, me], r_sem.at[v]).start()

        def one(d):
            t = z_order(d)
            pltpu.make_async_remote_copy(
                src_ref=src.at[v, pl.ds(t * 16, 16), :], dst_ref=dst.at[v, me],
                send_sem=s_sem.at[v], recv_sem=r_sem.at[v],
                device_id=z_peer(t), device_id_type=MESH,
            ).start()

        fold(15, one)

    def send_xy(src, dst, v, s_sem, r_sem):
        pltpu.make_async_copy(src.at[v, pl.ds(xy * 16, 16), :], dst.at[v, xy], r_sem.at[v]).start()

        def one(d):
            t = xy_order(d)
            pltpu.make_async_remote_copy(
                src_ref=src.at[v, pl.ds(t * 16, 16), :], dst_ref=dst.at[v, xy],
                send_sem=s_sem.at[v], recv_sem=r_sem.at[v],
                device_id=xy_peer(t), device_id_type=MESH,
            ).start()

        fold(15, one)

    def wait_all(ref, v, sem):
        pltpu.make_async_copy(ref.at[v], ref.at[v], sem.at[v]).wait()

    def wait_sent(ref, v, sem):
        part = ref.at[v, pl.ds(0, 15)]
        pltpu.make_async_copy(part, part, sem.at[v]).wait()

    def reorder(src, dst, v):
        rows = jnp.concatenate([src[v, s] for s in range(16)], axis=0)
        dst[v] = jnp.dot(perm[...], rows, preferred_element_type=F32).astype(BF16)

    def first_stage(along_z, src, dst, v, s_sem, r_sem):
        @pl.when(along_z)
        def _():
            send_z(src, dst, v, s_sem, r_sem)

        @pl.when(jnp.logical_not(along_z))
        def _():
            send_xy(src, dst, v, s_sem, r_sem)

    def start(v):
        first_stage(v % 2 == 0, y_send, a_recv, v, s_a, r_a)

    def forward(v):
        wait_all(a_recv, v, r_a)
        reorder(a_recv, b_send, v)
        first_stage(v % 2 == 1, b_send, r_recv, v, s_b, r_b)

    def rows_step(v):
        horizontal(v)

        @pl.when(v == 2)
        def _():
            pl.semaphore_wait(barrier, 31)
            start(0)
            start(1)

        @pl.when(v > 1)
        def _():
            start(v)

    fold(VL, rows_step)
    fold(VL, lambda i: forward(i + 1 - 2 * (i % 2)))

    def columns(v):
        wait_all(r_recv, v, r_b)
        rows = jnp.concatenate([r_recv[v, s] for s in range(16)], axis=0)
        tok[v] = jnp.dot(perm_in[v % 2], rows, preferred_element_type=F32).astype(BF16)
        at = pl.multiple_of(v * 256, 256)
        for p in range(2):
            project_to(
                1, tok[v, :, p * WIDTH : (p + 1) * WIDTH], [(2 * p, at), (2 * p + 1, at)]
            )

    fold(VL, columns)

    inner = slice(GROUP, GROUP + 256)

    def attend(v):
        at = pl.ds(pl.multiple_of(v * 256, 256), 256)
        for ln in range(4):
            attend_block(ln, at, q_s, k_s, va_s, m_s)
        for p in range(2):
            mixed = jnp.concatenate([m_s[2 * p, at, :], m_s[2 * p + 1, at, :]], axis=1)
            added = out_project(1, mixed)
            x = tok[v, :, p * WIDTH : (p + 1) * WIDTH].astype(F32)
            pad[v, p + 1, inner, :] = (x + added).astype(BF16)
        for copy in halos(v):
            copy.start()

    left = jnp.where(core == 0, far, near)
    right = jnp.where(core == 0, near, far)

    def halos(v):
        return (
            pltpu.make_async_remote_copy(
                src_ref=pad.at[v, 1, inner, :], dst_ref=pad.at[v, 3, inner, :],
                send_sem=s_h.at[v], recv_sem=r_h.at[v],
                device_id=(left, view), device_id_type=MESH,
            ),
            pltpu.make_async_remote_copy(
                src_ref=pad.at[v, 2, inner, :], dst_ref=pad.at[v, 0, inner, :],
                send_sem=s_g.at[v], recv_sem=r_g.at[v],
                device_id=(right, view), device_id_type=MESH,
            ),
        )

    block = place_xy * 2 + core
    has_left = jnp.where(block == 0, 0.0, 1.0).astype(F32)
    has_right = jnp.where(block == 31, 0.0, 1.0).astype(F32)
    place = lax.broadcasted_iota(jnp.int32, (GROUP, WIDTH), 0)

    lane = lax.broadcasted_iota(jnp.int32, (1, WIDTH), 1)
    keep_left = jnp.where(lane < CH, has_left, 1.0)
    keep_right = jnp.where(lane < CH, 1.0, has_right)

    def rims(ref, pairs):
        for p in range(pairs):
            last = pltpu.roll(ref[p, 8 * GROUP : 9 * GROUP, :].astype(F32), 2, 0)
            ref[p, 0:GROUP, :] = jnp.where(place < 2, 0.0, last).astype(BF16)
            head = pltpu.roll(ref[p, GROUP : 2 * GROUP, :].astype(F32), GROUP - 2, 0)
            ref[p, 9 * GROUP :, :] = jnp.where(place >= GROUP - 2, 0.0, head).astype(BF16)

    def taps(ref, pairs):
        return jnp.concatenate(
            [ref[p, dy * GROUP : dy * GROUP + 256, :] for dy in range(3) for p in pairs], axis=1
        )

    def leaky(got):
        return jnp.where(got >= 0, got, 0.1 * got)

    def convolve(v):
        for copy in halos(v):
            copy.wait()
        here = pad.at[v]
        here[0, inner, :] = (here[0, inner, :].astype(F32) * has_left).astype(BF16)
        here[3, inner, :] = (here[3, inner, :].astype(F32) * has_right).astype(BF16)
        rims(here, 4)
        got = leaky(jnp.dot(taps(here, (0, 1, 2)), w_c1[...], preferred_element_type=F32))
        hid[0, inner, :] = (got[:, 0:WIDTH] * keep_left).astype(BF16)
        hid[1, inner, :] = got[:, WIDTH:].astype(BF16)
        got = leaky(jnp.dot(taps(here, (2, 3)), w_c1b[...], preferred_element_type=F32))
        hid[2, inner, :] = (got * keep_right).astype(BF16)
        rims(hid, 3)
        got = jnp.dot(taps(hid, (0, 1, 2)), w_c2[...], preferred_element_type=F32)
        second = jnp.concatenate([here[1, inner, :], here[2, inner, :]], axis=1)
        result = (second.astype(F32) + got).astype(BF16)
        late = v // 3
        b2_send[v] = jnp.dot(perm_out[1 - late], result, preferred_element_type=F32).astype(BF16)
        first_stage(v < 3, b2_send, a2_recv, v, s_b2, r_b2)

    def back(v):
        wait_all(a2_recv, v, r_b2)
        reorder(a2_recv, y2_send, v)
        first_stage(v == 3, y2_send, f_recv, v, s_a2, r_a2)

    def columns_step(i):
        @pl.when(i < VL)
        def _():
            attend(i)

        @pl.when(i > 0)
        def _():
            convolve(i - 1)

    fold(VL + 1, columns_step)
    fold(VL, lambda i: back(i + i // 2 - 3 * (i // 3) + i // 3))

    def arrive(v):
        wait_all(f_recv, v, r_a2)
        rows = jnp.concatenate([f_recv[v, s] for s in range(16)], axis=0)
        got = jnp.dot(perm_end[v // 3], rows, preferred_element_type=F32).astype(BF16)
        for s in range(16):
            out_ref[v, s] = got[s * 16 : (s + 1) * 16, :]

    fold(VL, arrive)

    def drain(v):
        wait_sent(a_recv, v, s_a)
        wait_sent(r_recv, v, s_b)
        wait_sent(a2_recv, v, s_b2)
        wait_sent(f_recv, v, s_a2)

    fold(VL, drain)


def local(light_field, query_weight, key_weight, value_weight, out_weight, conv_first, conv_second):
    x = light_field.reshape(8, VL, 8192)
    vmem = pl.BlockSpec(memory_space=pltpu.VMEM)
    grid4 = pltpu.VMEM((VL, 16, 16, 256), BF16)
    flat4 = pltpu.VMEM((VL, 256, 256), BF16)
    sem = pltpu.SemaphoreType.DMA((VL,))
    weight = pltpu.VMEM((2, CH, WIDTH), BF16)
    taps = pltpu.VMEM((3, 3, CH, CH), BF16)
    got = pl.pallas_call(
        kernel,
        out_shape=jax.ShapeDtypeStruct((VL, 16, 16, 256), BF16),
        in_specs=[pl.BlockSpec(memory_space=pltpu.MemorySpace.HBM)] * 7,
        out_specs=vmem,
        scratch_shapes=[
            pltpu.VMEM((8, VL, 8192), BF16),
            weight, weight, weight, weight, taps, taps,
            pltpu.VMEM((2, TOK, WIDTH), F32),
            pltpu.VMEM((2, WIDTH, 6 * WIDTH), BF16),
            pltpu.VMEM((2, WIDTH, 2 * WIDTH), BF16),
            pltpu.VMEM((18 * CH, 4 * CH), BF16),
            pltpu.VMEM((12 * CH, 2 * CH), BF16),
            pltpu.VMEM((18 * CH, 4 * CH), BF16),
            pltpu.VMEM((2 * WIDTH, WIDTH), BF16),
            pltpu.VMEM((256, 256), BF16),
            pltpu.VMEM((2, 256, 256), BF16),
            pltpu.VMEM((2, 256, 256), BF16),
            pltpu.VMEM((2, 256, 256), BF16),
            pltpu.VMEM((4, TOK, WIDTH), BF16),
            pltpu.VMEM((4, TOK, WIDTH), BF16),
            pltpu.VMEM((4, TOK, 2 * WIDTH), BF16),
            pltpu.VMEM((4, TOK, WIDTH), BF16),
            flat4, grid4, flat4, grid4,
            flat4,
            pltpu.VMEM((VL, 4, 10 * GROUP, WIDTH), BF16),
            pltpu.VMEM((3, 10 * GROUP, WIDTH), BF16),
            flat4, grid4, flat4, grid4,
            pltpu.SemaphoreType.DMA((7,)),
            sem, sem, sem, sem, sem, sem, sem, sem, sem, sem, sem, sem,
        ],
        compiler_params=pltpu.CompilerParams(
            collective_id=0, has_side_effects=True, vmem_limit_bytes=62 << 20
        ),
    )(x, query_weight, key_weight, value_weight, out_weight.transpose(0, 2, 1), conv_first, conv_second)
    got = got.reshape(VL, 4, 2, 2, XY, 256).transpose(1, 3, 0, 4, 2, 5)
    return got.reshape(1, 8, VL, 8192)


def solution(mesh):
    placed = (P("line", None, "view", None), P(), P(), P(), P(), P(), P())
    return jax.shard_map(
        local, mesh=mesh, in_specs=placed, out_specs=P("line", None, "view", None), check_vma=False
    )
```

```python
import functools
import math

import jax
import jax.numpy as jnp
from jax import lax
from jax.experimental import pallas as pl
from jax.experimental.pallas import tpu as pltpu
from jax.sharding import PartitionSpec as P

F32 = jnp.float32
BF16 = jnp.bfloat16
MESH = pl.DeviceIdType.MESH

XY = 16
ZC = 16
VL = 4
CH = 64
WIDTH = 128
SCALE2 = math.log2(math.e) / math.sqrt(WIDTH)
GROUP = 32
TOK = 1024


def snake(t):
    y = t // 4
    x = t % 4
    return 4 * y + x + (y % 2) * (3 - 2 * x)


def fold(n, body):
    def step(i, carry):
        body(i)
        return carry

    lax.fori_loop(0, n, step, 0)


def normalise(x, avg):
    mean = jnp.dot(x, avg[0:WIDTH, :], preferred_element_type=F32)
    centre = x.astype(F32) - mean
    square = centre * centre
    high = square.astype(BF16)
    low = (square - high.astype(F32)).astype(BF16)
    spread = jnp.dot(
        jnp.concatenate([high, low], axis=1), avg[...], preferred_element_type=F32
    )
    return (centre * lax.rsqrt(spread + 1e-05)).astype(BF16)


def attend_block(line, at, q_s, k_s, va_s, m_s):
    scores = lax.dot_general(
        q_s[line, at, :], k_s[line], (((1,), (1,)), ((), ())), preferred_element_type=F32
    )
    top = jnp.max(scores, axis=1, keepdims=True)
    e = jnp.exp2((scores - top) * SCALE2).astype(BF16)
    o = jnp.dot(e, va_s[line], preferred_element_type=F32)
    m_s[line, at, :] = (o[:, :WIDTH] / o[:, WIDTH:]).astype(BF16)


def kernel(
    x_hbm, wq_hbm, wk_hbm, wv_hbm, wo_hbm, c1_hbm, c2_hbm, out_ref,
    x_in, wq_ref, wk_ref, wv_ref, wo_ref, c1_ref, c2_ref, x_rows,
    w_qkv, w_out, w_c1, w_c1b, w_c2, avg, perm, perm_in, perm_out, perm_end,
    q_s, k_s, va_s, m_s,
    y_send, a_recv, b_send, r_recv,
    tok, pad, hid,
    b2_send, a2_recv, y2_send, f_recv,
    l_sem, s_a, r_a, s_b, r_b, s_h, r_h, s_g, r_g, s_b2, r_b2, s_a2, r_a2,
):
    line = lax.axis_index("line")
    view = lax.axis_index("view")
    xy = line // 8
    zc = line % 8
    me = zc * 2 + view
    core = zc % 2
    z = (zc // 2) * 2 + view
    place_xy = snake(xy)
    far_xy = snake((place_xy + 15 + 2 * core) % 16)
    far = far_xy * 8 + zc + 1 - 2 * core
    near = line + 1 - 2 * core

    def z_peer(t):
        return (xy * 8 + t // 2, t % 2)

    def xy_peer(t):
        return (t * 8 + zc, view)

    def z_order(d):
        j = d // 2
        there = (z + 8 + (4 - (j + 1) // 2) * (2 * (j % 2) - 1)) % 8
        return (there // 2) * 4 + ((core + d + 1) % 2) * 2 + there % 2

    def hop(j):
        return (2 - j + (j // 2) * (2 * j - 1)) % 4

    def xy_order(d):
        return ((xy // 4 + hop(d // 4)) % 4) * 4 + (xy % 4 + hop(d % 4)) % 4

    barrier = pltpu.get_barrier_semaphore()

    def greet(d):
        pl.semaphore_signal(barrier, inc=1, device_id=z_peer(z_order(d)), device_id_type=MESH)
        pl.semaphore_signal(barrier, inc=1, device_id=xy_peer(xy_order(d)), device_id_type=MESH)

    fold(15, greet)
    pl.semaphore_signal(barrier, inc=1, device_id=(far, view), device_id_type=MESH)

    loads = [
        pltpu.make_async_copy(src, dst, l_sem.at[i])
        for i, (src, dst) in enumerate(
            (
                (x_hbm, x_in), (wq_hbm, wq_ref), (wk_hbm, wk_ref), (wv_hbm, wv_ref),
                (wo_hbm, wo_ref), (c1_hbm, c1_ref), (c2_hbm, c2_ref),
            )
        )
    ]
    for load in loads:
        load.start()
    for load in loads[:5]:
        load.wait()

    w_qkv[...] = jnp.zeros_like(w_qkv)
    w_out[...] = jnp.zeros_like(w_out)
    for i in range(2):
        for n, ref in enumerate((wq_ref, wk_ref, wv_ref)):
            for h in range(2):
                w_qkv[i, h * CH : (h + 1) * CH, (2 * n + h) * WIDTH : (2 * n + h + 1) * WIDTH] = ref[i]
        w_out[i, 0:CH, 0:WIDTH] = wo_ref[i]
        w_out[i, CH:, WIDTH:] = wo_ref[i]
    row = lax.broadcasted_iota(jnp.int32, (WIDTH, WIDTH), 0)
    col = lax.broadcasted_iota(jnp.int32, (WIDTH, WIDTH), 1)
    same = jnp.where((row < CH) == (col < CH), 1.0 / CH, 0.0).astype(BF16)
    avg[0:WIDTH, :] = same
    avg[WIDTH:, :] = same
    row = lax.broadcasted_iota(jnp.int32, (256, 256), 0)
    col = lax.broadcasted_iota(jnp.int32, (256, 256), 1)
    perm[...] = jnp.where(
        jnp.logical_and(row // 16 == col % 16, row % 16 == col // 16), 1.0, 0.0
    ).astype(BF16)
    for ln in range(4):
        va_s[ln, :, WIDTH:] = jnp.ones((TOK, WIDTH), BF16)

    def bring(t):
        for d in range(16):
            start = pl.multiple_of(snake(t) * 512 + (d // 2) % 2 * 256, 256)
            rays = x_in[(d // 4) * 2 + d % 2, :, pl.ds(start, 256)].astype(F32)
            for p in range(2):
                x_rows[p, pl.ds(d * 16 + t, VL, stride=256), :] = rays[:, p * WIDTH : (p + 1) * WIDTH]

    fold(16, bring)

    def project_to(i, pair, where):
        normed = normalise(pair, avg)
        rows = pair.shape[0]
        qkv = jnp.dot(normed, w_qkv[i], preferred_element_type=F32).astype(BF16)
        for h, (ln, start) in enumerate(where):
            at = pl.ds(start, rows)
            q_s[ln, at, :] = qkv[:, h * WIDTH : (h + 1) * WIDTH]
            k_s[ln, at, :] = qkv[:, (2 + h) * WIDTH : (3 + h) * WIDTH]
            va_s[ln, at, 0:WIDTH] = qkv[:, (4 + h) * WIDTH : (5 + h) * WIDTH]

    def out_project(i, mixed):
        return lax.dot_general(
            mixed, w_out[i], (((1,), (1,)), ((), ())), preferred_element_type=F32
        )

    def horizontal(v):
        at = pl.ds(pl.multiple_of(v * 256, 256), 256)
        for p in range(2):
            project_to(
                0, x_rows[p, at, :].astype(BF16), [(0, 2 * p * 256), (0, (2 * p + 1) * 256)]
            )
        for b in range(4):
            attend_block(0, slice(b * 256, (b + 1) * 256), q_s, k_s, va_s, m_s)
        for p in range(2):
            mixed = jnp.concatenate(
                [m_s[0, 2 * p * 256 : (2 * p + 1) * 256, :], m_s[0, (2 * p + 1) * 256 : (2 * p + 2) * 256, :]],
                axis=1,
            )
            added = out_project(0, mixed)
            y_send[v, :, p * WIDTH : (p + 1) * WIDTH] = (x_rows[p, at, :] + added).astype(BF16)

        @pl.when(v % 2 == 1)
        def _():
            y_send[v] = jnp.dot(perm[...], y_send[v], preferred_element_type=F32).astype(BF16)

    def send_z(src, dst, v, s_sem, r_sem):
        pltpu.make_async_copy(src.at[v, pl.ds(me * 16, 16), :], dst.at[v, me], r_sem.at[v]).start()

        def one(d):
            t = z_order(d)
            pltpu.make_async_remote_copy(
                src_ref=src.at[v, pl.ds(t * 16, 16), :], dst_ref=dst.at[v, me],
                send_sem=s_sem.at[v], recv_sem=r_sem.at[v],
                device_id=z_peer(t), device_id_type=MESH,
            ).start()

        fold(15, one)

    def send_xy(src, dst, v, s_sem, r_sem):
        pltpu.make_async_copy(src.at[v, pl.ds(xy * 16, 16), :], dst.at[v, xy], r_sem.at[v]).start()

        def one(d):
            t = xy_order(d)
            pltpu.make_async_remote_copy(
                src_ref=src.at[v, pl.ds(t * 16, 16), :], dst_ref=dst.at[v, xy],
                send_sem=s_sem.at[v], recv_sem=r_sem.at[v],
                device_id=xy_peer(t), device_id_type=MESH,
            ).start()

        fold(15, one)

    def wait_all(ref, v, sem):
        pltpu.make_async_copy(ref.at[v], ref.at[v], sem.at[v]).wait()

    def wait_sent(ref, v, sem):
        part = ref.at[v, pl.ds(0, 15)]
        pltpu.make_async_copy(part, part, sem.at[v]).wait()

    def reorder(src, dst, v):
        rows = jnp.concatenate([src[v, s] for s in range(16)], axis=0)
        dst[v] = jnp.dot(perm[...], rows, preferred_element_type=F32).astype(BF16)

    def first_stage(along_z, src, dst, v, s_sem, r_sem):
        @pl.when(along_z)
        def _():
            send_z(src, dst, v, s_sem, r_sem)

        @pl.when(jnp.logical_not(along_z))
        def _():
            send_xy(src, dst, v, s_sem, r_sem)

    def start(v):
        first_stage(v % 2 == 0, y_send, a_recv, v, s_a, r_a)

    def forward(v):
        wait_all(a_recv, v, r_a)
        reorder(a_recv, b_send, v)
        first_stage(v % 2 == 1, b_send, r_recv, v, s_b, r_b)

    def rows_step(v):
        horizontal(v)

        @pl.when(v == 1)
        def _():
            pl.semaphore_wait(barrier, 31)
            start(0)

        @pl.when(v > 0)
        def _():
            start(v)

    fold(VL, rows_step)
    for load in loads[5:]:
        load.wait()
    for ref, a, b in ((perm_in, row, col), (perm_out, col, row)):
        for odd in range(2):
            if odd:
                here = jnp.logical_and(a // 32 == b // 32, (a // 2) % 16 == b % 16)
                here = jnp.logical_and(here, a % 2 == (b // 16) % 2)
            else:
                here = jnp.logical_and(a // 32 == (b // 2) % 8, (a // 2) % 16 == b // 16)
                here = jnp.logical_and(here, a % 2 == b % 2)
            ref[odd] = jnp.where(here, 1.0, 0.0).astype(BF16)
    chip = snake(row % 16)
    for odd in range(2):
        if odd:
            here = jnp.logical_and(col % 16 == chip, col // 16 == row // 16)
        else:
            here = jnp.logical_and(col // 16 == chip, col % 16 == row // 16)
        perm_end[odd] = jnp.where(here, 1.0, 0.0).astype(BF16)
    none = jnp.zeros((CH, CH), BF16)
    for ref, dst, ins, outs in (
        (c1_ref, w_c1, range(-2, 4), range(-1, 3)),
        (c1_ref, w_c1b, range(2, 6), range(3, 5)),
        (c2_ref, w_c2, range(-1, 5), range(0, 4)),
    ):
        for dy in range(3):
            for i, c in enumerate(ins):
                row0 = (dy * len(ins) + i) * CH
                dst[row0 : row0 + CH, :] = jnp.concatenate(
                    [ref[dy, c - o + 1] if 0 <= c - o + 1 <= 2 else none for o in outs], axis=1
                )

    fold(VL, lambda i: forward(i + 1 - 2 * (i % 2)))

    def columns(v):
        wait_all(r_recv, v, r_b)
        rows = jnp.concatenate([r_recv[v, s] for s in range(16)], axis=0)
        tok[v] = jnp.dot(perm_in[v % 2], rows, preferred_element_type=F32).astype(BF16)
        at = pl.multiple_of(v * 256, 256)
        for p in range(2):
            project_to(
                1, tok[v, :, p * WIDTH : (p + 1) * WIDTH], [(2 * p, at), (2 * p + 1, at)]
            )

    fold(VL, columns)

    inner = slice(GROUP, GROUP + 256)

    def attend(v):
        at = pl.ds(pl.multiple_of(v * 256, 256), 256)
        for ln in range(4):
            attend_block(ln, at, q_s, k_s, va_s, m_s)
        for p in range(2):
            mixed = jnp.concatenate([m_s[2 * p, at, :], m_s[2 * p + 1, at, :]], axis=1)
            added = out_project(1, mixed)
            x = tok[v, :, p * WIDTH : (p + 1) * WIDTH].astype(F32)
            pad[v, p + 1, inner, :] = (x + added).astype(BF16)
        for copy in halos(v):
            copy.start()

    left = jnp.where(core == 0, far, near)
    right = jnp.where(core == 0, near, far)

    def halos(v):
        return (
            pltpu.make_async_remote_copy(
                src_ref=pad.at[v, 1, inner, :], dst_ref=pad.at[v, 3, inner, :],
                send_sem=s_h.at[v], recv_sem=r_h.at[v],
                device_id=(left, view), device_id_type=MESH,
            ),
            pltpu.make_async_remote_copy(
                src_ref=pad.at[v, 2, inner, :], dst_ref=pad.at[v, 0, inner, :],
                send_sem=s_g.at[v], recv_sem=r_g.at[v],
                device_id=(right, view), device_id_type=MESH,
            ),
        )

    block = place_xy * 2 + core
    has_left = jnp.where(block == 0, 0.0, 1.0).astype(F32)
    has_right = jnp.where(block == 31, 0.0, 1.0).astype(F32)
    place = lax.broadcasted_iota(jnp.int32, (GROUP, WIDTH), 0)

    lane = lax.broadcasted_iota(jnp.int32, (1, WIDTH), 1)
    keep_left = jnp.where(lane < CH, has_left, 1.0)
    keep_right = jnp.where(lane < CH, 1.0, has_right)

    def rims(ref, pairs):
        for p in range(pairs):
            last = pltpu.roll(ref[p, 8 * GROUP : 9 * GROUP, :].astype(F32), 2, 0)
            ref[p, 0:GROUP, :] = jnp.where(place < 2, 0.0, last).astype(BF16)
            head = pltpu.roll(ref[p, GROUP : 2 * GROUP, :].astype(F32), GROUP - 2, 0)
            ref[p, 9 * GROUP :, :] = jnp.where(place >= GROUP - 2, 0.0, head).astype(BF16)

    def taps(ref, pairs):
        return jnp.concatenate(
            [ref[p, dy * GROUP : dy * GROUP + 256, :] for dy in range(3) for p in pairs], axis=1
        )

    def leaky(got):
        return jnp.where(got >= 0, got, 0.1 * got)

    def convolve(v):
        for copy in halos(v):
            copy.wait()
        here = pad.at[v]
        here[0, inner, :] = (here[0, inner, :].astype(F32) * has_left).astype(BF16)
        here[3, inner, :] = (here[3, inner, :].astype(F32) * has_right).astype(BF16)
        rims(here, 4)
        got = leaky(jnp.dot(taps(here, (0, 1, 2)), w_c1[...], preferred_element_type=F32))
        hid[0, inner, :] = (got[:, 0:WIDTH] * keep_left).astype(BF16)
        hid[1, inner, :] = got[:, WIDTH:].astype(BF16)
        got = leaky(jnp.dot(taps(here, (2, 3)), w_c1b[...], preferred_element_type=F32))
        hid[2, inner, :] = (got * keep_right).astype(BF16)
        rims(hid, 3)
        got = jnp.dot(taps(hid, (0, 1, 2)), w_c2[...], preferred_element_type=F32)
        second = jnp.concatenate([here[1, inner, :], here[2, inner, :]], axis=1)
        result = (second.astype(F32) + got).astype(BF16)
        late = v // 3
        b2_send[v] = jnp.dot(perm_out[1 - late], result, preferred_element_type=F32).astype(BF16)
        first_stage(v < 3, b2_send, a2_recv, v, s_b2, r_b2)

    def back(v):
        wait_all(a2_recv, v, r_b2)
        reorder(a2_recv, y2_send, v)
        first_stage(v == 3, y2_send, f_recv, v, s_a2, r_a2)

    def columns_step(i):
        @pl.when(i < VL)
        def _():
            attend(i)

        @pl.when(i > 0)
        def _():
            convolve(i - 1)

    fold(VL + 1, columns_step)
    fold(VL, lambda i: back(i + i // 2 - 3 * (i // 3) + i // 3))

    def arrive(v):
        wait_all(f_recv, v, r_a2)
        rows = jnp.concatenate([f_recv[v, s] for s in range(16)], axis=0)
        got = jnp.dot(perm_end[v // 3], rows, preferred_element_type=F32).astype(BF16)
        for s in range(16):
            out_ref[v, s] = got[s * 16 : (s + 1) * 16, :]

    fold(VL, arrive)

    def drain(v):
        wait_sent(a_recv, v, s_a)
        wait_sent(r_recv, v, s_b)
        wait_sent(a2_recv, v, s_b2)
        wait_sent(f_recv, v, s_a2)

    fold(VL, drain)


def local(light_field, query_weight, key_weight, value_weight, out_weight, conv_first, conv_second):
    x = light_field.reshape(8, VL, 8192)
    operands = (
        x, query_weight, key_weight, value_weight, out_weight.transpose(0, 2, 1), conv_first, conv_second
    )
    vmem = pl.BlockSpec(memory_space=pltpu.VMEM)
    grid4 = pltpu.VMEM((VL, 16, 16, 256), BF16)
    flat4 = pltpu.VMEM((VL, 256, 256), BF16)
    sem = pltpu.SemaphoreType.DMA((VL,))
    weight = pltpu.VMEM((2, CH, WIDTH), BF16)
    taps = pltpu.VMEM((3, 3, CH, CH), BF16)
    got = pl.pallas_call(
        kernel,
        out_shape=jax.ShapeDtypeStruct((VL, 16, 16, 256), BF16),
        in_specs=[pl.BlockSpec(memory_space=pltpu.MemorySpace.HBM)] * 7,
        out_specs=vmem,
        scratch_shapes=[
            pltpu.VMEM((8, VL, 8192), BF16),
            weight, weight, weight, weight, taps, taps,
            pltpu.VMEM((2, TOK, WIDTH), F32),
            pltpu.VMEM((2, WIDTH, 6 * WIDTH), BF16),
            pltpu.VMEM((2, WIDTH, 2 * WIDTH), BF16),
            pltpu.VMEM((18 * CH, 4 * CH), BF16),
            pltpu.VMEM((12 * CH, 2 * CH), BF16),
            pltpu.VMEM((18 * CH, 4 * CH), BF16),
            pltpu.VMEM((2 * WIDTH, WIDTH), BF16),
            pltpu.VMEM((256, 256), BF16),
            pltpu.VMEM((2, 256, 256), BF16),
            pltpu.VMEM((2, 256, 256), BF16),
            pltpu.VMEM((2, 256, 256), BF16),
            pltpu.VMEM((4, TOK, WIDTH), BF16),
            pltpu.VMEM((4, TOK, WIDTH), BF16),
            pltpu.VMEM((4, TOK, 2 * WIDTH), BF16),
            pltpu.VMEM((4, TOK, WIDTH), BF16),
            flat4, grid4, flat4, grid4,
            flat4,
            pltpu.VMEM((VL, 4, 10 * GROUP, WIDTH), BF16),
            pltpu.VMEM((3, 10 * GROUP, WIDTH), BF16),
            flat4, grid4, flat4, grid4,
            pltpu.SemaphoreType.DMA((7,)),
            sem, sem, sem, sem, sem, sem, sem, sem, sem, sem, sem, sem,
        ],
        compiler_params=pltpu.CompilerParams(
            collective_id=0, has_side_effects=True, vmem_limit_bytes=48 << 20
        ),
    )(*[pltpu.with_memory_space_constraint(a, pltpu.MemorySpace.HBM) for a in operands])
    got = got.reshape(VL, 4, 2, 2, XY, 256).transpose(1, 3, 0, 4, 2, 5)
    return got.reshape(1, 8, VL, 8192)


def solution(mesh):
    placed = (P("line", None, "view", None), P(), P(), P(), P(), P(), P())
    return jax.shard_map(
        local, mesh=mesh, in_specs=placed, out_specs=P("line", None, "view", None), check_vma=False
    )
```

```python
import functools
import math

import jax
import jax.numpy as jnp
from jax import lax
from jax.experimental import pallas as pl
from jax.experimental.pallas import tpu as pltpu
from jax.sharding import PartitionSpec as P

F32 = jnp.float32
BF16 = jnp.bfloat16
MESH = pl.DeviceIdType.MESH

XY = 16
ZC = 16
VL = 4
CH = 64
WIDTH = 128
SCALE2 = math.log2(math.e) / math.sqrt(WIDTH)
GROUP = 32
TOK = 1024


def snake(t):
    y = t // 4
    x = t % 4
    return 4 * y + x + (y % 2) * (3 - 2 * x)


def fold(n, body):
    def step(i, carry):
        body(i)
        return carry

    lax.fori_loop(0, n, step, 0)


def normalise(x, avg):
    mean = jnp.dot(x, avg[0:WIDTH, :], preferred_element_type=F32)
    centre = x.astype(F32) - mean
    square = centre * centre
    high = square.astype(BF16)
    low = (square - high.astype(F32)).astype(BF16)
    spread = jnp.dot(
        jnp.concatenate([high, low], axis=1), avg[...], preferred_element_type=F32
    )
    return (centre * lax.rsqrt(spread + 1e-05)).astype(BF16)


def attend_block(line, at, q_s, k_s, va_s, m_s):
    scores = lax.dot_general(
        q_s[line, at, :], k_s[line], (((1,), (1,)), ((), ())), preferred_element_type=F32
    )
    top = jnp.max(scores, axis=1, keepdims=True)
    e = jnp.exp2((scores - top) * SCALE2).astype(BF16)
    o = jnp.dot(e, va_s[line], preferred_element_type=F32)
    m_s[line, at, :] = (o[:, :WIDTH] / o[:, WIDTH:]).astype(BF16)


def kernel(
    x_hbm, wq_hbm, wk_hbm, wv_hbm, wo_hbm, c1_hbm, c2_hbm, out_ref,
    x_in, wq_ref, wk_ref, wv_ref, wo_ref, c1_ref, c2_ref, x_rows,
    w_qkv, w_out, w_c1, w_c1b, w_c2, avg, perm, perm_in, perm_out, perm_end,
    q_s, k_s, va_s, m_s,
    y_send, a_recv, b_send, r_recv,
    tok, pad, hid,
    b2_send, a2_recv, y2_send, f_recv,
    l_sem, s_a, r_a, s_b, r_b, s_h, r_h, s_g, r_g, s_b2, r_b2, s_a2, r_a2,
):
    line = lax.axis_index("line")
    view = lax.axis_index("view")
    xy = line // 8
    zc = line % 8
    me = zc * 2 + view
    core = zc % 2
    z = (zc // 2) * 2 + view
    place_xy = snake(xy)
    far_xy = snake((place_xy + 15 + 2 * core) % 16)
    far = far_xy * 8 + zc + 1 - 2 * core
    near = line + 1 - 2 * core

    def z_peer(t):
        return (xy * 8 + t // 2, t % 2)

    def xy_peer(t):
        return (t * 8 + zc, view)

    def z_order(d):
        j = d // 2
        there = (z + 8 + (4 - (j + 1) // 2) * (2 * (j % 2) - 1)) % 8
        return (there // 2) * 4 + ((core + d + 1) % 2) * 2 + there % 2

    def hop(j):
        return (2 - j + (j // 2) * (2 * j - 1)) % 4

    def xy_order(d):
        return ((xy // 4 + hop(d // 4)) % 4) * 4 + (xy % 4 + hop(d % 4)) % 4

    barrier = pltpu.get_barrier_semaphore()

    def greet(d):
        pl.semaphore_signal(barrier, inc=1, device_id=z_peer(z_order(d)), device_id_type=MESH)
        pl.semaphore_signal(barrier, inc=1, device_id=xy_peer(xy_order(d)), device_id_type=MESH)

    fold(15, greet)
    pl.semaphore_signal(barrier, inc=1, device_id=(far, view), device_id_type=MESH)

    loads = [
        pltpu.make_async_copy(src, dst, l_sem.at[i])
        for i, (src, dst) in enumerate(
            (
                (x_hbm, x_in), (wq_hbm, wq_ref), (wk_hbm, wk_ref), (wv_hbm, wv_ref),
                (wo_hbm, wo_ref), (c1_hbm, c1_ref), (c2_hbm, c2_ref),
            )
        )
    ]
    for load in loads:
        load.start()
    for load in loads[:5]:
        load.wait()

    w_qkv[...] = jnp.zeros_like(w_qkv)
    w_out[...] = jnp.zeros_like(w_out)
    for i in range(2):
        for n, ref in enumerate((wq_ref, wk_ref, wv_ref)):
            for h in range(2):
                w_qkv[i, h * CH : (h + 1) * CH, (2 * n + h) * WIDTH : (2 * n + h + 1) * WIDTH] = ref[i]
        w_out[i, 0:CH, 0:WIDTH] = wo_ref[i]
        w_out[i, CH:, WIDTH:] = wo_ref[i]
    row = lax.broadcasted_iota(jnp.int32, (WIDTH, WIDTH), 0)
    col = lax.broadcasted_iota(jnp.int32, (WIDTH, WIDTH), 1)
    same = jnp.where((row < CH) == (col < CH), 1.0 / CH, 0.0).astype(BF16)
    avg[0:WIDTH, :] = same
    avg[WIDTH:, :] = same
    row = lax.broadcasted_iota(jnp.int32, (256, 256), 0)
    col = lax.broadcasted_iota(jnp.int32, (256, 256), 1)
    perm[...] = jnp.where(
        jnp.logical_and(row // 16 == col % 16, row % 16 == col // 16), 1.0, 0.0
    ).astype(BF16)
    for ln in range(4):
        va_s[ln, :, WIDTH:] = jnp.ones((TOK, WIDTH), BF16)

    def bring(t):
        for d in range(16):
            start = pl.multiple_of(snake(t) * 512 + (d // 2) % 2 * 256, 256)
            rays = x_in[(d // 4) * 2 + d % 2, :, pl.ds(start, 256)].astype(F32)
            for p in range(2):
                x_rows[p, pl.ds(d * 16 + t, VL, stride=256), :] = rays[:, p * WIDTH : (p + 1) * WIDTH]

    fold(16, bring)

    def project_to(i, pair, where):
        normed = normalise(pair, avg)
        rows = pair.shape[0]
        qkv = jnp.dot(normed, w_qkv[i], preferred_element_type=F32).astype(BF16)
        for h, (ln, start) in enumerate(where):
            at = pl.ds(start, rows)
            q_s[ln, at, :] = qkv[:, h * WIDTH : (h + 1) * WIDTH]
            k_s[ln, at, :] = qkv[:, (2 + h) * WIDTH : (3 + h) * WIDTH]
            va_s[ln, at, 0:WIDTH] = qkv[:, (4 + h) * WIDTH : (5 + h) * WIDTH]

    def out_project(i, mixed):
        return lax.dot_general(
            mixed, w_out[i], (((1,), (1,)), ((), ())), preferred_element_type=F32
        )

    def horizontal(v):
        at = pl.ds(pl.multiple_of(v * 256, 256), 256)
        for p in range(2):
            project_to(
                0, x_rows[p, at, :].astype(BF16), [(0, 2 * p * 256), (0, (2 * p + 1) * 256)]
            )
        for b in range(4):
            attend_block(0, slice(b * 256, (b + 1) * 256), q_s, k_s, va_s, m_s)
        for p in range(2):
            mixed = jnp.concatenate(
                [m_s[0, 2 * p * 256 : (2 * p + 1) * 256, :], m_s[0, (2 * p + 1) * 256 : (2 * p + 2) * 256, :]],
                axis=1,
            )
            added = out_project(0, mixed)
            y_send[v, :, p * WIDTH : (p + 1) * WIDTH] = (x_rows[p, at, :] + added).astype(BF16)

        @pl.when(v % 2 == 1)
        def _():
            y_send[v] = jnp.dot(perm[...], y_send[v], preferred_element_type=F32).astype(BF16)

    def send_z(src, dst, v, s_sem, r_sem):
        pltpu.make_async_copy(src.at[v, pl.ds(me * 16, 16), :], dst.at[v, me], r_sem.at[v]).start()

        def one(d):
            t = z_order(d)
            pltpu.make_async_remote_copy(
                src_ref=src.at[v, pl.ds(t * 16, 16), :], dst_ref=dst.at[v, me],
                send_sem=s_sem.at[v], recv_sem=r_sem.at[v],
                device_id=z_peer(t), device_id_type=MESH,
            ).start()

        fold(15, one)

    def send_xy(src, dst, v, s_sem, r_sem):
        pltpu.make_async_copy(src.at[v, pl.ds(xy * 16, 16), :], dst.at[v, xy], r_sem.at[v]).start()

        def one(d):
            t = xy_order(d)
            pltpu.make_async_remote_copy(
                src_ref=src.at[v, pl.ds(t * 16, 16), :], dst_ref=dst.at[v, xy],
                send_sem=s_sem.at[v], recv_sem=r_sem.at[v],
                device_id=xy_peer(t), device_id_type=MESH,
            ).start()

        fold(15, one)

    def wait_all(ref, v, sem):
        pltpu.make_async_copy(ref.at[v], ref.at[v], sem.at[v]).wait()

    def wait_sent(ref, v, sem):
        part = ref.at[v, pl.ds(0, 15)]
        pltpu.make_async_copy(part, part, sem.at[v]).wait()

    def reorder(src, dst, v):
        rows = jnp.concatenate([src[v, s] for s in range(16)], axis=0)
        dst[v] = jnp.dot(perm[...], rows, preferred_element_type=F32).astype(BF16)

    def first_stage(along_z, src, dst, v, s_sem, r_sem):
        @pl.when(along_z)
        def _():
            send_z(src, dst, v, s_sem, r_sem)

        @pl.when(jnp.logical_not(along_z))
        def _():
            send_xy(src, dst, v, s_sem, r_sem)

    def start(v):
        first_stage(v % 2 == 0, y_send, a_recv, v, s_a, r_a)

    def forward(v):
        wait_all(a_recv, v, r_a)
        reorder(a_recv, b_send, v)
        first_stage(v % 2 == 1, b_send, r_recv, v, s_b, r_b)

    def rows_step(v):
        horizontal(v)

        @pl.when(v == 1)
        def _():
            pl.semaphore_wait(barrier, 31)
            start(0)

        @pl.when(v > 0)
        def _():
            start(v)

    fold(VL, rows_step)
    for load in loads[5:]:
        load.wait()
    for ref, a, b in ((perm_in, row, col), (perm_out, col, row)):
        for odd in range(2):
            if odd:
                here = jnp.logical_and(a // 32 == b // 32, (a // 2) % 16 == b % 16)
                here = jnp.logical_and(here, a % 2 == (b // 16) % 2)
            else:
                here = jnp.logical_and(a // 32 == (b // 2) % 8, (a // 2) % 16 == b // 16)
                here = jnp.logical_and(here, a % 2 == b % 2)
            ref[odd] = jnp.where(here, 1.0, 0.0).astype(BF16)
    chip = snake(row % 16)
    for odd in range(2):
        if odd:
            here = jnp.logical_and(col % 16 == chip, col // 16 == row // 16)
        else:
            here = jnp.logical_and(col // 16 == chip, col % 16 == row // 16)
        perm_end[odd] = jnp.where(here, 1.0, 0.0).astype(BF16)
    none = jnp.zeros((CH, CH), BF16)
    for ref, dst, ins, outs in (
        (c1_ref, w_c1, range(-2, 4), range(-1, 3)),
        (c1_ref, w_c1b, range(2, 6), range(3, 5)),
        (c2_ref, w_c2, range(-1, 5), range(0, 4)),
    ):
        for dy in range(3):
            for i, c in enumerate(ins):
                row0 = (dy * len(ins) + i) * CH
                dst[row0 : row0 + CH, :] = jnp.concatenate(
                    [ref[dy, c - o + 1] if 0 <= c - o + 1 <= 2 else none for o in outs], axis=1
                )

    fold(VL, lambda i: forward(i + (1 - 2 * i) * (1 - i // 2)))

    def columns(v):
        wait_all(r_recv, v, r_b)
        rows = jnp.concatenate([r_recv[v, s] for s in range(16)], axis=0)
        tok[v] = jnp.dot(perm_in[v % 2], rows, preferred_element_type=F32).astype(BF16)
        at = pl.multiple_of(v * 256, 256)
        for p in range(2):
            project_to(
                1, tok[v, :, p * WIDTH : (p + 1) * WIDTH], [(2 * p, at), (2 * p + 1, at)]
            )

    fold(VL, columns)

    inner = slice(GROUP, GROUP + 256)

    def attend(v):
        at = pl.ds(pl.multiple_of(v * 256, 256), 256)
        for ln in range(4):
            attend_block(ln, at, q_s, k_s, va_s, m_s)

    def join(v):
        at = pl.ds(pl.multiple_of(v * 256, 256), 256)
        for p in range(2):
            mixed = jnp.concatenate([m_s[2 * p, at, :], m_s[2 * p + 1, at, :]], axis=1)
            added = out_project(1, mixed)
            x = tok[v, :, p * WIDTH : (p + 1) * WIDTH].astype(F32)
            pad[v, p + 1, inner, :] = (x + added).astype(BF16)
        for copy in halos(v):
            copy.start()

    left = jnp.where(core == 0, far, near)
    right = jnp.where(core == 0, near, far)

    def halos(v):
        return (
            pltpu.make_async_remote_copy(
                src_ref=pad.at[v, 1, inner, :], dst_ref=pad.at[v, 3, inner, :],
                send_sem=s_h.at[v], recv_sem=r_h.at[v],
                device_id=(left, view), device_id_type=MESH,
            ),
            pltpu.make_async_remote_copy(
                src_ref=pad.at[v, 2, inner, :], dst_ref=pad.at[v, 0, inner, :],
                send_sem=s_g.at[v], recv_sem=r_g.at[v],
                device_id=(right, view), device_id_type=MESH,
            ),
        )

    block = place_xy * 2 + core
    has_left = jnp.where(block == 0, 0.0, 1.0).astype(F32)
    has_right = jnp.where(block == 31, 0.0, 1.0).astype(F32)
    place = lax.broadcasted_iota(jnp.int32, (GROUP, WIDTH), 0)

    lane = lax.broadcasted_iota(jnp.int32, (1, WIDTH), 1)
    keep_left = jnp.where(lane < CH, has_left, 1.0)
    keep_right = jnp.where(lane < CH, 1.0, has_right)

    def rims(ref, pairs):
        for p in range(pairs):
            last = pltpu.roll(ref[p, 8 * GROUP : 9 * GROUP, :].astype(F32), 2, 0)
            ref[p, 0:GROUP, :] = jnp.where(place < 2, 0.0, last).astype(BF16)
            head = pltpu.roll(ref[p, GROUP : 2 * GROUP, :].astype(F32), GROUP - 2, 0)
            ref[p, 9 * GROUP :, :] = jnp.where(place >= GROUP - 2, 0.0, head).astype(BF16)

    def taps(ref, pairs):
        return jnp.concatenate(
            [ref[p, dy * GROUP : dy * GROUP + 256, :] for dy in range(3) for p in pairs], axis=1
        )

    def leaky(got):
        return jnp.where(got >= 0, got, 0.1 * got)

    def meet(v):
        for copy in halos(v):
            copy.wait()

    def convolve(v):
        here = pad.at[v]
        here[0, inner, :] = (here[0, inner, :].astype(F32) * has_left).astype(BF16)
        here[3, inner, :] = (here[3, inner, :].astype(F32) * has_right).astype(BF16)
        rims(here, 4)
        got = leaky(jnp.dot(taps(here, (0, 1, 2)), w_c1[...], preferred_element_type=F32))
        hid[0, inner, :] = (got[:, 0:WIDTH] * keep_left).astype(BF16)
        hid[1, inner, :] = got[:, WIDTH:].astype(BF16)
        got = leaky(jnp.dot(taps(here, (2, 3)), w_c1b[...], preferred_element_type=F32))
        hid[2, inner, :] = (got * keep_right).astype(BF16)
        rims(hid, 3)
        got = jnp.dot(taps(hid, (0, 1, 2)), w_c2[...], preferred_element_type=F32)
        second = jnp.concatenate([here[1, inner, :], here[2, inner, :]], axis=1)
        result = (second.astype(F32) + got).astype(BF16)
        late = v // 3
        b2_send[v] = jnp.dot(perm_out[1 - late], result, preferred_element_type=F32).astype(BF16)

    def leave(v):
        first_stage(v < 3, b2_send, a2_recv, v, s_b2, r_b2)

    def back(v):
        wait_all(a2_recv, v, r_b2)
        reorder(a2_recv, y2_send, v)
        first_stage(v == 3, y2_send, f_recv, v, s_a2, r_a2)

    def columns_start(v):
        attend(v)
        join(v)

    fold(2, columns_start)

    def columns_step(i):
        meet(i)
        attend(i + 2)
        convolve(i)
        join(i + 2)
        leave(i)

    fold(2, columns_step)

    def columns_end(i):
        meet(i + 2)
        convolve(i + 2)
        leave(i + 2)

    fold(2, columns_end)
    fold(VL, lambda i: back(i + i // 2 - 3 * (i // 3) + i // 3))

    def arrive(v):
        wait_all(f_recv, v, r_a2)
        rows = jnp.concatenate([f_recv[v, s] for s in range(16)], axis=0)
        got = jnp.dot(perm_end[v // 3], rows, preferred_element_type=F32).astype(BF16)
        for s in range(16):
            out_ref[v, s] = got[s * 16 : (s + 1) * 16, :]

    fold(VL, arrive)

    def drain(v):
        wait_sent(a_recv, v, s_a)
        wait_sent(r_recv, v, s_b)
        wait_sent(a2_recv, v, s_b2)
        wait_sent(f_recv, v, s_a2)

    fold(VL, drain)


def local(light_field, query_weight, key_weight, value_weight, out_weight, conv_first, conv_second):
    x = light_field.reshape(8, VL, 8192)
    operands = (
        x, query_weight, key_weight, value_weight, out_weight.transpose(0, 2, 1), conv_first, conv_second
    )
    vmem = pl.BlockSpec(memory_space=pltpu.VMEM)
    grid4 = pltpu.VMEM((VL, 16, 16, 256), BF16)
    flat4 = pltpu.VMEM((VL, 256, 256), BF16)
    sem = pltpu.SemaphoreType.DMA((VL,))
    weight = pltpu.VMEM((2, CH, WIDTH), BF16)
    taps = pltpu.VMEM((3, 3, CH, CH), BF16)
    got = pl.pallas_call(
        kernel,
        out_shape=jax.ShapeDtypeStruct((VL, 16, 16, 256), BF16),
        in_specs=[pl.BlockSpec(memory_space=pltpu.MemorySpace.HBM)] * 7,
        out_specs=vmem,
        scratch_shapes=[
            pltpu.VMEM((8, VL, 8192), BF16),
            weight, weight, weight, weight, taps, taps,
            pltpu.VMEM((2, TOK, WIDTH), F32),
            pltpu.VMEM((2, WIDTH, 6 * WIDTH), BF16),
            pltpu.VMEM((2, WIDTH, 2 * WIDTH), BF16),
            pltpu.VMEM((18 * CH, 4 * CH), BF16),
            pltpu.VMEM((12 * CH, 2 * CH), BF16),
            pltpu.VMEM((18 * CH, 4 * CH), BF16),
            pltpu.VMEM((2 * WIDTH, WIDTH), BF16),
            pltpu.VMEM((256, 256), BF16),
            pltpu.VMEM((2, 256, 256), BF16),
            pltpu.VMEM((2, 256, 256), BF16),
            pltpu.VMEM((2, 256, 256), BF16),
            pltpu.VMEM((4, TOK, WIDTH), BF16),
            pltpu.VMEM((4, TOK, WIDTH), BF16),
            pltpu.VMEM((4, TOK, 2 * WIDTH), BF16),
            pltpu.VMEM((4, TOK, WIDTH), BF16),
            flat4, grid4, flat4, grid4,
            flat4,
            pltpu.VMEM((VL, 4, 10 * GROUP, WIDTH), BF16),
            pltpu.VMEM((3, 10 * GROUP, WIDTH), BF16),
            flat4, grid4, flat4, grid4,
            pltpu.SemaphoreType.DMA((7,)),
            sem, sem, sem, sem, sem, sem, sem, sem, sem, sem, sem, sem,
        ],
        compiler_params=pltpu.CompilerParams(
            collective_id=0, has_side_effects=True, vmem_limit_bytes=48 << 20
        ),
    )(*[pltpu.with_memory_space_constraint(a, pltpu.MemorySpace.HBM) for a in operands])
    got = got.reshape(VL, 4, 2, 2, XY, 256).transpose(1, 3, 0, 4, 2, 5)
    return got.reshape(1, 8, VL, 8192)


def solution(mesh):
    placed = (P("line", None, "view", None), P(), P(), P(), P(), P(), P())
    return jax.shard_map(
        local, mesh=mesh, in_specs=placed, out_specs=P("line", None, "view", None), check_vma=False
    )
```

```python
import functools
import math

import jax
import jax.numpy as jnp
from jax import lax
from jax.experimental import pallas as pl
from jax.experimental.pallas import tpu as pltpu
from jax.sharding import PartitionSpec as P

F32 = jnp.float32
BF16 = jnp.bfloat16
MESH = pl.DeviceIdType.MESH

XY = 16
ZC = 16
VL = 4
CH = 64
WIDTH = 128
SCALE2 = math.log2(math.e) / math.sqrt(WIDTH)
GROUP = 32
TOK = 1024


def snake(t):
    y = t // 4
    x = t % 4
    return 4 * y + x + (y % 2) * (3 - 2 * x)


def fold(n, body):
    def step(i, carry):
        body(i)
        return carry

    lax.fori_loop(0, n, step, 0)


def normalise(x, avg):
    mean = jnp.dot(x, avg[0:WIDTH, :], preferred_element_type=F32)
    centre = x.astype(F32) - mean
    square = centre * centre
    high = square.astype(BF16)
    low = (square - high.astype(F32)).astype(BF16)
    spread = jnp.dot(
        jnp.concatenate([high, low], axis=1), avg[...], preferred_element_type=F32
    )
    return (centre * lax.rsqrt(spread + 1e-05)).astype(BF16)


def attend_block(line, at, q_s, k_s, va_s, m_s):
    scores = lax.dot_general(
        q_s[line, at, :], k_s[line], (((1,), (1,)), ((), ())), preferred_element_type=F32
    )
    top = jnp.max(scores, axis=1, keepdims=True)
    e = jnp.exp2((scores - top) * SCALE2).astype(BF16)
    o = jnp.dot(e, va_s[line], preferred_element_type=F32)
    m_s[line, at, :] = (o[:, :WIDTH] / o[:, WIDTH:]).astype(BF16)


def kernel(
    x_hbm, wq_hbm, wk_hbm, wv_hbm, wo_hbm, c1_hbm, c2_hbm, out_ref,
    x_in, wq_ref, wk_ref, wv_ref, wo_ref, c1_ref, c2_ref, x_rows,
    w_qkv, w_out, w_c1, w_c1b, w_c2, avg, perm, perm_in, perm_out, perm_end,
    q_s, k_s, va_s, m_s,
    y_send, a_recv, b_send, r_recv,
    tok, pad, hid,
    b2_send, a2_recv, y2_send, f_recv,
    l_sem, s_a, r_a, s_b, r_b, s_h, r_h, s_g, r_g, s_b2, r_b2, s_a2, r_a2,
):
    line = lax.axis_index("line")
    view = lax.axis_index("view")
    xy = line // 8
    zc = line % 8
    me = zc * 2 + view
    core = zc % 2
    z = (zc // 2) * 2 + view
    place_xy = snake(xy)
    far_xy = snake((place_xy + 15 + 2 * core) % 16)
    far = far_xy * 8 + zc + 1 - 2 * core
    near = line + 1 - 2 * core

    def z_peer(t):
        return (xy * 8 + t // 2, t % 2)

    def xy_peer(t):
        return (t * 8 + zc, view)

    def z_order(d):
        j = d // 2
        there = (z + 8 + (4 - (j + 1) // 2) * (2 * (j % 2) - 1)) % 8
        return (there // 2) * 4 + ((core + d + 1) % 2) * 2 + there % 2

    def hop(j):
        return (2 - j + (j // 2) * (2 * j - 1)) % 4

    def xy_order(d):
        return ((xy // 4 + hop(d // 4)) % 4) * 4 + (xy % 4 + hop(d % 4)) % 4

    barrier = pltpu.get_barrier_semaphore()

    def greet(d):
        pl.semaphore_signal(barrier, inc=1, device_id=z_peer(z_order(d)), device_id_type=MESH)
        pl.semaphore_signal(barrier, inc=1, device_id=xy_peer(xy_order(d)), device_id_type=MESH)

    fold(15, greet)
    pl.semaphore_signal(barrier, inc=1, device_id=(far, view), device_id_type=MESH)

    loads = [
        pltpu.make_async_copy(src, dst, l_sem.at[i])
        for i, (src, dst) in enumerate(
            (
                (x_hbm, x_in), (wq_hbm, wq_ref), (wk_hbm, wk_ref), (wv_hbm, wv_ref),
                (wo_hbm, wo_ref), (c1_hbm, c1_ref), (c2_hbm, c2_ref),
            )
        )
    ]
    for load in loads:
        load.start()
    for load in loads[:5]:
        load.wait()

    w_qkv[...] = jnp.zeros_like(w_qkv)
    w_out[...] = jnp.zeros_like(w_out)
    for i in range(2):
        for n, ref in enumerate((wq_ref, wk_ref, wv_ref)):
            for h in range(2):
                w_qkv[i, h * CH : (h + 1) * CH, (2 * n + h) * WIDTH : (2 * n + h + 1) * WIDTH] = ref[i]
        w_out[i, 0:CH, 0:WIDTH] = wo_ref[i]
        w_out[i, CH:, WIDTH:] = wo_ref[i]
    row = lax.broadcasted_iota(jnp.int32, (WIDTH, WIDTH), 0)
    col = lax.broadcasted_iota(jnp.int32, (WIDTH, WIDTH), 1)
    same = jnp.where((row < CH) == (col < CH), 1.0 / CH, 0.0).astype(BF16)
    avg[0:WIDTH, :] = same
    avg[WIDTH:, :] = same
    row = lax.broadcasted_iota(jnp.int32, (256, 256), 0)
    col = lax.broadcasted_iota(jnp.int32, (256, 256), 1)
    perm[...] = jnp.where(
        jnp.logical_and(row // 16 == col % 16, row % 16 == col // 16), 1.0, 0.0
    ).astype(BF16)
    for ln in range(4):
        va_s[ln, :, WIDTH:] = jnp.ones((TOK, WIDTH), BF16)

    def bring(t):
        for d in range(16):
            start = pl.multiple_of(snake(t) * 512 + (d // 2) % 2 * 256, 256)
            rays = x_in[(d // 4) * 2 + d % 2, :, pl.ds(start, 256)].astype(F32)
            for p in range(2):
                x_rows[p, pl.ds(d * 16 + t, VL, stride=256), :] = rays[:, p * WIDTH : (p + 1) * WIDTH]

    fold(16, bring)

    def project_to(i, pair, where):
        normed = normalise(pair, avg)
        rows = pair.shape[0]
        qkv = jnp.dot(normed, w_qkv[i], preferred_element_type=F32).astype(BF16)
        for h, (ln, start) in enumerate(where):
            at = pl.ds(start, rows)
            q_s[ln, at, :] = qkv[:, h * WIDTH : (h + 1) * WIDTH]
            k_s[ln, at, :] = qkv[:, (2 + h) * WIDTH : (3 + h) * WIDTH]
            va_s[ln, at, 0:WIDTH] = qkv[:, (4 + h) * WIDTH : (5 + h) * WIDTH]

    def out_project(i, mixed):
        return lax.dot_general(
            mixed, w_out[i], (((1,), (1,)), ((), ())), preferred_element_type=F32
        )

    def horizontal(v):
        at = pl.ds(pl.multiple_of(v * 256, 256), 256)
        for p in range(2):
            project_to(
                0, x_rows[p, at, :].astype(BF16), [(0, 2 * p * 256), (0, (2 * p + 1) * 256)]
            )
        for b in range(4):
            attend_block(0, slice(b * 256, (b + 1) * 256), q_s, k_s, va_s, m_s)
        for p in range(2):
            mixed = jnp.concatenate(
                [m_s[0, 2 * p * 256 : (2 * p + 1) * 256, :], m_s[0, (2 * p + 1) * 256 : (2 * p + 2) * 256, :]],
                axis=1,
            )
            added = out_project(0, mixed)
            y_send[v, :, p * WIDTH : (p + 1) * WIDTH] = (x_rows[p, at, :] + added).astype(BF16)

        @pl.when(v % 2 == 1)
        def _():
            y_send[v] = jnp.dot(perm[...], y_send[v], preferred_element_type=F32).astype(BF16)

    def send_z(src, dst, v, s_sem, r_sem):
        pltpu.make_async_copy(src.at[v, pl.ds(me * 16, 16), :], dst.at[v, me], r_sem.at[v]).start()

        def one(d):
            t = z_order(d)
            pltpu.make_async_remote_copy(
                src_ref=src.at[v, pl.ds(t * 16, 16), :], dst_ref=dst.at[v, me],
                send_sem=s_sem.at[v], recv_sem=r_sem.at[v],
                device_id=z_peer(t), device_id_type=MESH,
            ).start()

        fold(15, one)

    def send_xy(src, dst, v, s_sem, r_sem):
        pltpu.make_async_copy(src.at[v, pl.ds(xy * 16, 16), :], dst.at[v, xy], r_sem.at[v]).start()

        def one(d):
            t = xy_order(d)
            pltpu.make_async_remote_copy(
                src_ref=src.at[v, pl.ds(t * 16, 16), :], dst_ref=dst.at[v, xy],
                send_sem=s_sem.at[v], recv_sem=r_sem.at[v],
                device_id=xy_peer(t), device_id_type=MESH,
            ).start()

        fold(15, one)

    def wait_all(ref, v, sem):
        pltpu.make_async_copy(ref.at[v], ref.at[v], sem.at[v]).wait()

    def wait_sent(ref, v, sem):
        part = ref.at[v, pl.ds(0, 15)]
        pltpu.make_async_copy(part, part, sem.at[v]).wait()

    def reorder(src, dst, v):
        rows = jnp.concatenate([src[v, s] for s in range(16)], axis=0)
        dst[v] = jnp.dot(perm[...], rows, preferred_element_type=F32).astype(BF16)

    def first_stage(along_z, src, dst, v, s_sem, r_sem):
        @pl.when(along_z)
        def _():
            send_z(src, dst, v, s_sem, r_sem)

        @pl.when(jnp.logical_not(along_z))
        def _():
            send_xy(src, dst, v, s_sem, r_sem)

    def start(v):
        first_stage(v % 2 == 0, y_send, a_recv, v, s_a, r_a)

    def forward(v):
        wait_all(a_recv, v, r_a)
        reorder(a_recv, b_send, v)
        first_stage(v % 2 == 1, b_send, r_recv, v, s_b, r_b)

    def rows_step(v):
        horizontal(v)

        @pl.when(v == 1)
        def _():
            pl.semaphore_wait(barrier, 31)
            start(0)

        @pl.when(v > 0)
        def _():
            start(v)

    fold(VL, rows_step)
    for load in loads[5:]:
        load.wait()
    for ref, a, b in ((perm_in, row, col), (perm_out, col, row)):
        for odd in range(2):
            if odd:
                here = jnp.logical_and(a // 32 == b // 32, (a // 2) % 16 == b % 16)
                here = jnp.logical_and(here, a % 2 == (b // 16) % 2)
            else:
                here = jnp.logical_and(a // 32 == (b // 2) % 8, (a // 2) % 16 == b // 16)
                here = jnp.logical_and(here, a % 2 == b % 2)
            ref[odd] = jnp.where(here, 1.0, 0.0).astype(BF16)
    chip = snake((row // 2) % 16)
    device = row // 64 * 4 + row % 2 * 2 + (row // 32) % 2
    for odd in range(2):
        if odd:
            here = jnp.logical_and(col % 16 == chip, col // 16 == device)
        else:
            here = jnp.logical_and(col // 16 == chip, col % 16 == device)
        perm_end[odd] = jnp.where(here, 1.0, 0.0).astype(BF16)
    none = jnp.zeros((CH, CH), BF16)
    for ref, dst, ins, outs in (
        (c1_ref, w_c1, range(-2, 4), range(-1, 3)),
        (c1_ref, w_c1b, range(2, 6), range(3, 5)),
        (c2_ref, w_c2, range(-1, 5), range(0, 4)),
    ):
        for dy in range(3):
            for i, c in enumerate(ins):
                row0 = (dy * len(ins) + i) * CH
                dst[row0 : row0 + CH, :] = jnp.concatenate(
                    [ref[dy, c - o + 1] if 0 <= c - o + 1 <= 2 else none for o in outs], axis=1
                )

    fold(VL, lambda i: forward(i + (1 - 2 * i) * (1 - i // 2)))

    def columns(v):
        wait_all(r_recv, v, r_b)
        rows = jnp.concatenate([r_recv[v, s] for s in range(16)], axis=0)
        tok[v] = jnp.dot(perm_in[v % 2], rows, preferred_element_type=F32).astype(BF16)
        at = pl.multiple_of(v * 256, 256)
        for p in range(2):
            project_to(
                1, tok[v, :, p * WIDTH : (p + 1) * WIDTH], [(2 * p, at), (2 * p + 1, at)]
            )

    fold(VL, columns)

    inner = slice(GROUP, GROUP + 256)

    def attend(v):
        at = pl.ds(pl.multiple_of(v * 256, 256), 256)
        for ln in range(4):
            attend_block(ln, at, q_s, k_s, va_s, m_s)

    def join(v):
        at = pl.ds(pl.multiple_of(v * 256, 256), 256)
        for p in range(2):
            mixed = jnp.concatenate([m_s[2 * p, at, :], m_s[2 * p + 1, at, :]], axis=1)
            added = out_project(1, mixed)
            x = tok[v, :, p * WIDTH : (p + 1) * WIDTH].astype(F32)
            pad[v, p + 1, inner, :] = (x + added).astype(BF16)
        for copy in halos(v):
            copy.start()

    left = jnp.where(core == 0, far, near)
    right = jnp.where(core == 0, near, far)

    def halos(v):
        return (
            pltpu.make_async_remote_copy(
                src_ref=pad.at[v, 1, inner, :], dst_ref=pad.at[v, 3, inner, :],
                send_sem=s_h.at[v], recv_sem=r_h.at[v],
                device_id=(left, view), device_id_type=MESH,
            ),
            pltpu.make_async_remote_copy(
                src_ref=pad.at[v, 2, inner, :], dst_ref=pad.at[v, 0, inner, :],
                send_sem=s_g.at[v], recv_sem=r_g.at[v],
                device_id=(right, view), device_id_type=MESH,
            ),
        )

    block = place_xy * 2 + core
    has_left = jnp.where(block == 0, 0.0, 1.0).astype(F32)
    has_right = jnp.where(block == 31, 0.0, 1.0).astype(F32)
    place = lax.broadcasted_iota(jnp.int32, (GROUP, WIDTH), 0)

    lane = lax.broadcasted_iota(jnp.int32, (1, WIDTH), 1)
    keep_left = jnp.where(lane < CH, has_left, 1.0)
    keep_right = jnp.where(lane < CH, 1.0, has_right)

    def rims(ref, pairs):
        for p in range(pairs):
            last = pltpu.roll(ref[p, 8 * GROUP : 9 * GROUP, :].astype(F32), 2, 0)
            ref[p, 0:GROUP, :] = jnp.where(place < 2, 0.0, last).astype(BF16)
            head = pltpu.roll(ref[p, GROUP : 2 * GROUP, :].astype(F32), GROUP - 2, 0)
            ref[p, 9 * GROUP :, :] = jnp.where(place >= GROUP - 2, 0.0, head).astype(BF16)

    def taps(ref, pairs):
        return jnp.concatenate(
            [ref[p, dy * GROUP : dy * GROUP + 256, :] for dy in range(3) for p in pairs], axis=1
        )

    def leaky(got):
        return jnp.where(got >= 0, got, 0.1 * got)

    def meet(v):
        for copy in halos(v):
            copy.wait()

    def convolve(v):
        here = pad.at[v]
        here[0, inner, :] = (here[0, inner, :].astype(F32) * has_left).astype(BF16)
        here[3, inner, :] = (here[3, inner, :].astype(F32) * has_right).astype(BF16)
        rims(here, 4)
        got = leaky(jnp.dot(taps(here, (0, 1, 2)), w_c1[...], preferred_element_type=F32))
        hid[0, inner, :] = (got[:, 0:WIDTH] * keep_left).astype(BF16)
        hid[1, inner, :] = got[:, WIDTH:].astype(BF16)
        got = leaky(jnp.dot(taps(here, (2, 3)), w_c1b[...], preferred_element_type=F32))
        hid[2, inner, :] = (got * keep_right).astype(BF16)
        rims(hid, 3)
        got = jnp.dot(taps(hid, (0, 1, 2)), w_c2[...], preferred_element_type=F32)
        second = jnp.concatenate([here[1, inner, :], here[2, inner, :]], axis=1)
        result = (second.astype(F32) + got).astype(BF16)
        late = v // 3
        b2_send[v] = jnp.dot(perm_out[1 - late], result, preferred_element_type=F32).astype(BF16)

    def leave(v):
        first_stage(v < 3, b2_send, a2_recv, v, s_b2, r_b2)

    def back(v):
        wait_all(a2_recv, v, r_b2)
        reorder(a2_recv, y2_send, v)
        first_stage(v == 3, y2_send, f_recv, v, s_a2, r_a2)

    def columns_start(v):
        attend(v)
        join(v)

    fold(2, columns_start)

    def columns_step(i):
        meet(i)
        attend(i + 2)
        convolve(i)
        join(i + 2)
        leave(i)

    fold(2, columns_step)

    def columns_end(i):
        meet(i + 2)
        convolve(i + 2)
        leave(i + 2)

    fold(2, columns_end)
    fold(VL, lambda i: back(i + i // 2 - 3 * (i // 3) + i // 3))

    def arrive(v):
        wait_all(f_recv, v, r_a2)
        rows = jnp.concatenate([f_recv[v, s] for s in range(16)], axis=0)
        got = jnp.dot(perm_end[v // 3], rows, preferred_element_type=F32).astype(BF16)
        for u in range(8):
            out_ref[u, v] = got[u * 32 : (u + 1) * 32, :]

    fold(VL, arrive)

    def drain(v):
        wait_sent(a_recv, v, s_a)
        wait_sent(r_recv, v, s_b)
        wait_sent(a2_recv, v, s_b2)
        wait_sent(f_recv, v, s_a2)

    fold(VL, drain)


def local(light_field, query_weight, key_weight, value_weight, out_weight, conv_first, conv_second):
    x = light_field.reshape(8, VL, 8192)
    operands = (
        x, query_weight, key_weight, value_weight, out_weight.transpose(0, 2, 1), conv_first, conv_second
    )
    vmem = pl.BlockSpec(memory_space=pltpu.VMEM)
    grid4 = pltpu.VMEM((VL, 16, 16, 256), BF16)
    flat4 = pltpu.VMEM((VL, 256, 256), BF16)
    sem = pltpu.SemaphoreType.DMA((VL,))
    weight = pltpu.VMEM((2, CH, WIDTH), BF16)
    taps = pltpu.VMEM((3, 3, CH, CH), BF16)
    got = pl.pallas_call(
        kernel,
        out_shape=jax.ShapeDtypeStruct((8, VL, 32, 256), BF16),
        in_specs=[pl.BlockSpec(memory_space=pltpu.MemorySpace.HBM)] * 7,
        out_specs=vmem,
        scratch_shapes=[
            pltpu.VMEM((8, VL, 8192), BF16),
            weight, weight, weight, weight, taps, taps,
            pltpu.VMEM((2, TOK, WIDTH), F32),
            pltpu.VMEM((2, WIDTH, 6 * WIDTH), BF16),
            pltpu.VMEM((2, WIDTH, 2 * WIDTH), BF16),
            pltpu.VMEM((18 * CH, 4 * CH), BF16),
            pltpu.VMEM((12 * CH, 2 * CH), BF16),
            pltpu.VMEM((18 * CH, 4 * CH), BF16),
            pltpu.VMEM((2 * WIDTH, WIDTH), BF16),
            pltpu.VMEM((256, 256), BF16),
            pltpu.VMEM((2, 256, 256), BF16),
            pltpu.VMEM((2, 256, 256), BF16),
            pltpu.VMEM((2, 256, 256), BF16),
            pltpu.VMEM((4, TOK, WIDTH), BF16),
            pltpu.VMEM((4, TOK, WIDTH), BF16),
            pltpu.VMEM((4, TOK, 2 * WIDTH), BF16),
            pltpu.VMEM((4, TOK, WIDTH), BF16),
            flat4, grid4, flat4, grid4,
            flat4,
            pltpu.VMEM((VL, 4, 10 * GROUP, WIDTH), BF16),
            pltpu.VMEM((3, 10 * GROUP, WIDTH), BF16),
            flat4, grid4, flat4, grid4,
            pltpu.SemaphoreType.DMA((7,)),
            sem, sem, sem, sem, sem, sem, sem, sem, sem, sem, sem, sem,
        ],
        compiler_params=pltpu.CompilerParams(
            collective_id=0, has_side_effects=True, vmem_limit_bytes=48 << 20
        ),
    )(*[pltpu.with_memory_space_constraint(a, pltpu.MemorySpace.HBM) for a in operands])
    return got.reshape(1, 8, VL, 8192)


def solution(mesh):
    placed = (P("line", None, "view", None), P(), P(), P(), P(), P(), P())
    return jax.shard_map(
        local, mesh=mesh, in_specs=placed, out_specs=P("line", None, "view", None), check_vma=False
    )
```
